512 devices in a mesh: ctx: 32 (over y, x), mp: 16 (over z, core).
Axes of the slice: x: 4, y: 8, z: 8, core: 2. Of those that a mesh axis runs over, the one named last changes fastest.
Arguments:
- source_rows: bfloat16 [16384, 3, 8192], P('ctx', None, 'mp'), may hold values from -6 to 6
- short_filters: bfloat16 [3, 7, 8192], P(None, None, 'mp'), may hold values from -2 to 2
- medium_filters: bfloat16 [128, 512], P(None, 'mp'), may hold values from -0.5 to 0.5
- skip_gain: float32 [8192], P('mp'), may hold values from 0.1 to 1.9
- out_weight: bfloat16 [8192, 8192], P('mp', 'ctx'), may hold values from -0.0625 to 0.0625
- doc_lengths: int32 [8], replicated, may hold values from 1 to 2048, 8192 in all
- block_packing_device: int32 [32, 16], replicated, may hold values from 0 to 31, as said below
Outputs:
- mixed: bfloat16 [8192, 8192], P('ctx', 'mp')
The draws below stay inside these ranges and needn't reach their ends.
Inputs may be any that keep to these rules, and one draw needn't show every extreme that they name: `block_packing_device`: row c names, for the 16 blocks of stretch c in order, the packing device that holds each; the entries of one row differ, and some packing device is named in every row. A packing device keeps the blocks it holds in increasing order of their stretch, in its first slots.
All inputs are finite; a program needn't handle non-finite values.
Results may differ from the reference program's by a relative error of at most 0.02.
Values may be sent and summed in bfloat16 or wider, within the bound.
No kernel may reach another device: no remote copies, remote signals or barrier semaphores. Data moves between devices by JAX's collectives and lax.ppermute only.
A program may use at most 128 MiB of HBM per device.

```python
import math
import jax
import jax.numpy as jnp
import numpy as np
from jax import lax

D = 8192
GROUPS = 512
SE_LEN = 7
MR_LEN = 128
DOCS = 8
STRETCHES = 32
NB_OWN = 16
BLK = 16
SRC_ROWS = 512
TOKENS = 8192
WIDTH_DEV = 512
DOC_MOST = 2048


def draw_block_packing_device(key, part):
    base = jax.random.fold_in(key, 11)
    key_heavy, key_bias, key_score = jax.random.split(base, 3)
    heavy_blocks = jax.random.randint(key_heavy, (), 0, STRETCHES)
    level_values = jax.random.randint(key_bias, (STRETCHES,), 0, 4)
    random_noise = jax.random.randint(key_score, (STRETCHES, STRETCHES), 0, 4096)
    block_owners = jnp.arange(STRETCHES, dtype=jnp.int32)
    extra_reward = jnp.where(block_owners == heavy_blocks, 100000, 0).astype(jnp.int32)
    block_score = random_noise + level_values[None, :] * 1024 + extra_reward[None, :]
    block_score = block_score * STRETCHES + block_owners[None, :]
    picked = lax.top_k(block_score, NB_OWN)[1]
    return picked.astype(jnp.int32)


def level_of(rng, extent, pieces, smallest, top_value):
    def one(dim, blocks):
        heights = jax.random.uniform(jax.random.fold_in(jax.random.fold_in(rng, 6), dim), (blocks,), jnp.float32, smallest / len(pieces), top_value / len(pieces))
        return jnp.repeat(jnp.exp(heights), extent[dim] // blocks).reshape((-1,) + (1,) * (len(extent) - dim - 1))

    gain = one(*pieces[0])
    for cut in pieces[1:]:
        gain = gain * one(*cut)
    return gain


def profile(count, total, bound, lean):
    loads = [(1 << 20) // math.isqrt(standing ** lean) + 1 for standing in range(2, count + 1)]
    rest, counts = total - bound - (count - 1), [1] * (count - 1)
    while rest > 0:
        candidates = [i for i in range(count - 1) if counts[i] < bound]
        whole, remaining = sum([loads[i] for i in candidates]), rest
        for i in candidates:
            addition = min(bound - counts[i], max(1, remaining * loads[i] // whole), rest)
            counts[i] = counts[i] + addition
            rest = rest - addition
    return np.array([bound] + counts)


def ragged_sizes(own_key, amount, total, limit, slope):
    if amount == 2:
        one = jax.random.randint(own_key, (), max(1, total - limit), min(limit, total - 1) + 1)
        return jnp.stack([one, total - one])
    lengths = jnp.asarray(profile(amount, total, limit, slope), jnp.int32)
    couples = (amount - 1) // 2
    source_of, receiver = lengths[1:1 + 2 * couples:2], lengths[2:2 + 2 * couples:2]
    room = jnp.minimum(source_of - 1, limit - receiver)
    moved = jax.random.randint(jax.random.fold_in(own_key, 1), (couples,), 0, 1 << 20) % (room + 1)
    lengths = lengths.at[1:1 + 2 * couples:2].set(source_of - moved).at[2:2 + 2 * couples:2].set(receiver + moved)
    return lengths[jax.random.permutation(jax.random.fold_in(own_key, 2), amount)]


def noise(rng, dims, width, limit, shards=(), held_as=jnp.bfloat16):
    array = width * jax.random.normal(rng, dims, jnp.float32)
    if shards:
        array = array * level_of(rng, dims, shards, -0.22, 0.18)
    return jnp.clip(array, -limit, limit).astype(held_as)


def setup_inputs(seed: int = 0) -> dict:
    keys = jax.random.split(jax.random.key(seed), 8)
    source_rows = noise(keys[0], (STRETCHES * SRC_ROWS, 3, D), 1.0, 6.0, ((0, 32), (2, 16)))
    short_filters = noise(keys[1], (3, SE_LEN, D), SE_LEN ** -0.5, 2.0, ((2, 16),))
    medium_filters = noise(keys[2], (MR_LEN, GROUPS), MR_LEN ** -0.5, 0.5, ((1, 16),))
    skip_gain = jnp.clip(1.0 + 0.18 * jax.random.normal(keys[3], (D,), jnp.float32), 0.1, 1.9)
    out_weight = noise(keys[4], (D, D), D ** -0.5, 0.0625, ((0, 16), (1, 32)))
    doc_lengths = ragged_sizes(keys[5], DOCS, TOKENS, DOC_MOST, 2).astype(jnp.int32)
    block_packing_device = draw_block_packing_device(jax.random.fold_in(keys[7], 71), 0)
    return {"source_rows": source_rows, "short_filters": short_filters, "medium_filters": medium_filters, "skip_gain": skip_gain, "out_weight": out_weight, "doc_lengths": doc_lengths, "block_packing_device": block_packing_device}


def short_conv(data, filt, back):
    rows = data.shape[0]
    padded = jnp.pad(data.astype(jnp.float32), ((SE_LEN - 1, 0), (0, 0)))
    taps = filt.astype(jnp.float32)
    total = jnp.zeros((rows, data.shape[1]), jnp.float32)
    for step in range(SE_LEN):
        keep = (back >= step).astype(jnp.float32)[:, None]
        piece = padded[SE_LEN - 1 - step:SE_LEN - 1 - step + rows]
        total = total + taps[step][None, :] * piece * keep
    return total


def reference(source_rows, short_filters, medium_filters, skip_gain, out_weight, doc_lengths, block_packing_device):
    ends = jnp.cumsum(doc_lengths).astype(jnp.int32)
    starts = (ends - doc_lengths).astype(jnp.int32)
    where_row = jnp.arange(TOKENS, dtype=jnp.int32)
    begin = jnp.max(jnp.where(starts[None, :] <= where_row[:, None], starts[None, :], 0), axis=1).astype(jnp.int32)
    back = (where_row - begin).astype(jnp.int32)
    block_owners = jnp.arange(STRETCHES, dtype=jnp.int32)
    member = jnp.any(block_packing_device[:, :, None] == block_owners[None, None, :], axis=1).astype(jnp.int32)
    before = (jnp.cumsum(member, axis=0) - member).astype(jnp.int32)
    ranks = jnp.take_along_axis(before, block_packing_device, axis=1).astype(jnp.int32)
    first = (block_packing_device * SRC_ROWS + ranks * BLK).reshape(-1).astype(jnp.int32)
    index_rows = (first[:, None] + jnp.arange(BLK, dtype=jnp.int32)[None, :]).reshape(-1).astype(jnp.int32)
    packed = jnp.take(source_rows, index_rows, axis=0)
    query = short_conv(packed[:, 0], short_filters[0], back)
    keyed = short_conv(packed[:, 1], short_filters[1], back)
    valued = short_conv(packed[:, 2], short_filters[2], back)
    z_vals = (keyed * valued).astype(jnp.bfloat16)
    z_wide = z_vals.astype(jnp.float32)
    zpad = jnp.pad(z_wide, ((MR_LEN - 1, 0), (0, 0)))
    taps = jnp.repeat(medium_filters.astype(jnp.float32), D // GROUPS, axis=1)

    def add_tap(step, total):
        step = jnp.asarray(step).astype(jnp.int32)
        offset = (MR_LEN - 1 - step).astype(jnp.int32)
        piece = lax.dynamic_slice_in_dim(zpad, offset, TOKENS, 0)
        tap = lax.dynamic_slice_in_dim(taps, step, 1, 0)
        keep = (back >= step).astype(jnp.float32)[:, None]
        return total + tap * piece * keep

    medium = lax.fori_loop(0, MR_LEN, add_tap, jnp.zeros((TOKENS, D), jnp.float32))
    hidden = (query * (medium + skip_gain[None, :] * z_wide)).astype(jnp.bfloat16)
    mixed = jnp.zeros((TOKENS, D), jnp.float32)
    for block in range(D // WIDTH_DEV):
        lo = block * WIDTH_DEV
        part = jnp.dot(hidden[:, lo:lo + WIDTH_DEV], out_weight[lo:lo + WIDTH_DEV], preferred_element_type=jnp.float32)
        part = lax.optimization_barrier(part.astype(jnp.bfloat16))
        mixed = mixed + part.astype(jnp.float32)
    return mixed.astype(jnp.bfloat16)
```

```python
import functools

import jax
import jax.numpy as jnp
from jax import lax
from jax.experimental import pallas as pl
from jax.experimental.pallas import tpu as pltpu
from jax.sharding import Mesh, PartitionSpec as P

CTX = ("y", "x")
SHAPE4 = (8, 4, 8, 2)
BLK = 16
TAIL = 8
HALF = 128
F32, BF16 = jnp.float32, jnp.bfloat16


def smem():
    return pl.BlockSpec(memory_space=pltpu.SMEM)


def vmem():
    return pl.BlockSpec(memory_space=pltpu.VMEM)


def stretch_id():
    return lax.axis_index("y") * lax.axis_size("x") + lax.axis_index("x")


def call(body, outs, ins, args, flops, scratch=(), name=None):
    moved = sum(a.size * a.dtype.itemsize for a in args)
    moved += sum(o.size * o.dtype.itemsize for o in outs)
    return pl.pallas_call(
        body,
        out_shape=outs,
        in_specs=ins,
        out_specs=[vmem()] * len(outs),
        scratch_shapes=list(scratch),
        cost_estimate=pl.CostEstimate(flops=flops, bytes_accessed=moved, transcendentals=0),
        name=name,
    )(*args)


def reach_back(lengths, first, shape):
    at = first + lax.broadcasted_iota(jnp.int32, shape, 0)
    begin = jnp.zeros(shape, jnp.int32)
    start = jnp.int32(0)
    for doc in range(lengths.shape[0]):
        begin = jnp.where(at >= start, start, begin)
        start = start + lengths[doc]
    return at - begin


def short_rows(window, taps_ref, which, back):
    count = back.shape[0]
    total = jnp.zeros(back.shape, F32)
    for step in range(taps_ref.shape[1]):
        tap = taps_ref[which, step : step + 1, :].astype(F32)
        piece = window[TAIL - step : TAIL - step + count]
        total = total + jnp.where(back >= step, tap * piece, 0.0)
    return total


def pack_kernel(bpd, src, kv, q):
    me = stretch_id()

    def one(c, slot):
        mine = jnp.int32(0)
        for k in range(bpd.shape[1]):
            mine = mine | (bpd[c, k] == me).astype(jnp.int32)
        rows = pl.ds(pl.multiple_of(slot * BLK, BLK), BLK)
        kv[c, 0] = src[1, rows, :]
        kv[c, 1] = src[2, rows, :]
        q[c] = src[0, rows, :]
        return slot + mine

    lax.fori_loop(0, bpd.shape[0], one, jnp.int32(0))


def toeplitz_kernel(line, out):
    def one(g, carry):
        row = jnp.broadcast_to(line[pl.ds(g, 1), :], out.shape[1:])
        out[g] = pltpu.roll(row, 0, 1, stride=1, stride_axis=0).astype(BF16)
        return carry

    lax.fori_loop(0, out.shape[0], one, 0)


def z_kernel(bpd, lengths, kv, taps, z, send, head, buf):
    me = stretch_id()
    rows, width = z.shape
    for i in range(2):
        buf[i, 0:TAIL, :] = jnp.zeros((TAIL, width), F32)
    for k in range(rows // BLK):
        s = bpd[me, k]
        for i in range(2):
            buf[i, TAIL + k * BLK : TAIL + (k + 1) * BLK, :] = kv[s, i].astype(F32)

    step = 32

    def chunk(r, carry):
        at = pl.multiple_of(r * step, step)
        back = reach_back(lengths, me * rows + at, (step, width))
        wide = pl.ds(at, step + TAIL)
        keyed = short_rows(buf[0, wide, :], taps, 1, back)
        valued = short_rows(buf[1, wide, :], taps, 2, back)
        z[pl.ds(at, step), :] = (keyed * valued).astype(BF16)
        return carry

    lax.fori_loop(0, rows // step, chunk, 0)
    send[0:HALF, :] = z[rows - HALF :, :]
    for i in range(2):
        send[HALF + i * TAIL : HALF + (i + 1) * TAIL, :] = buf[i, rows : rows + TAIL, :].astype(BF16)
        head[i * TAIL : (i + 1) * TAIL, :] = buf[i, TAIL : 2 * TAIL, :].astype(BF16)


def medium_kernel(lengths, z, recv, head, taps, bands, gain, out, ext):
    me = stretch_id()
    rows, width = z.shape
    back = reach_back(lengths, me * rows, (TAIL, width))
    fixed = []
    for i in range(2):
        tail = recv[HALF + i * TAIL : HALF + (i + 1) * TAIL, :].astype(F32)
        mine = head[i * TAIL : (i + 1) * TAIL, :].astype(F32)
        fixed.append(short_rows(jnp.concatenate([tail, mine], axis=0), taps, 1 + i, back))
    first = (fixed[0] * fixed[1]).astype(BF16).astype(F32)
    ext[0:HALF, :] = recv[0:HALF, :]
    ext[HALF:, :] = z[...]
    later = z[TAIL : 2 * TAIL, :].astype(F32)
    ext[HALF : HALF + 2 * TAIL, :] = jnp.concatenate([first, later], axis=0).astype(BF16)
    lane = 128
    per = lane // (width // bands.shape[0])
    group = lax.broadcasted_iota(jnp.int32, (HALF, lane), 1) // (lane // per)
    for b in range(rows // HALF):
        back = reach_back(lengths, me * rows + b * HALF, (HALF, 2 * HALF))
        i = lax.broadcasted_iota(jnp.int32, (HALF, 2 * HALF), 0)
        p = lax.broadcasted_iota(jnp.int32, (HALF, 2 * HALF), 1)
        keep = jnp.where(i + HALF - p <= back, 1.0, 0.0).astype(BF16)
        for t in range(width // lane):
            cols = slice(t * lane, (t + 1) * lane)
            right = ext[b * HALF : (b + 2) * HALF, cols]
            total = jnp.zeros((HALF, lane), F32)
            for g in range(per):
                got = jnp.dot(bands[t * per + g] * keep, right, preferred_element_type=F32)
                total = jnp.where(group == g, got, total)
            zs = ext[(b + 1) * HALF : (b + 2) * HALF, cols].astype(F32)
            out[b * HALF : (b + 1) * HALF, cols] = total + gain[:, cols] * zs


def hidden_kernel(half, bpd, lengths, q, halo, taps, medium, out, buf):
    me = stretch_id()
    width = medium.shape[1]
    rows = medium.shape[0]
    if half == 0:
        buf[0:TAIL, :] = halo[...].astype(F32)
    else:
        s = bpd[me, half * HALF // BLK - 1]
        buf[0:TAIL, :] = q[s].astype(F32)[BLK - TAIL :]
    for k in range(HALF // BLK):
        s = bpd[me, half * HALF // BLK + k]
        buf[TAIL + k * BLK : TAIL + (k + 1) * BLK, :] = q[s].astype(F32)
    step = 32

    def chunk(r, carry):
        at = pl.multiple_of(r * step, step)
        first = half * HALF + at
        back = reach_back(lengths, me * rows + first, (step, width))
        query = short_rows(buf[pl.ds(at, step + TAIL), :], taps, 0, back)
        value = (query * medium[pl.ds(pl.multiple_of(first, step), step), :]).astype(BF16)
        for copy in range(out.shape[0]):
            out[copy, pl.ds(at, step), :] = value
        return carry

    lax.fori_loop(0, HALF // step, chunk, 0)


def project_kernel(own, other, weight, out):
    k = own.shape[1]
    lane = out.shape[2]
    step = 256

    def rows(r, carry):
        at = pl.ds(pl.multiple_of(r * step, step), step)
        for pair in range(out.shape[0] // 2):
            cols = slice(pair * 2 * lane, (pair + 1) * 2 * lane)
            got = jnp.dot(own[at, :], weight[0:k, cols], preferred_element_type=F32)
            got = got + jnp.dot(other[at, :], weight[k:, cols], preferred_element_type=F32)
            got = got.astype(BF16)
            out[2 * pair, at, :] = got[:, :lane]
            out[2 * pair + 1, at, :] = got[:, lane:]
        return carry

    lax.fori_loop(0, own.shape[0] // step, rows, 0)


def shape(dims, dtype=BF16):
    return jax.ShapeDtypeStruct(dims, dtype)


def passed_along(block):
    n = lax.axis_size(CTX)
    return lax.ppermute(block, CTX, [(i, i + 1) for i in range(n - 1)])


def weight_columns(out_weight):
    nx = lax.axis_size("x")
    core = lax.axis_index("core")
    width = out_weight.shape[1] // 2
    halves = (out_weight[:, :width], out_weight[:, width:])
    same = jnp.where(core == 0, halves[0], halves[1])
    flip = jnp.where(core == 0, halves[1], halves[0])
    route = lambda f: [
        (x * 2 + i, (2 * (x % 2) + f(i)) * 2 + x // 2) for x in range(nx) for i in range(2)
    ]
    a = lax.ppermute(same, ("x", "core"), route(lambda i: i))
    b = lax.ppermute(flip, ("x", "core"), route(lambda i: 1 - i))
    straight = lax.axis_index("x") % 2 == core
    own = jnp.where(straight, a, b)
    other = jnp.where(straight, b, a)
    both = jnp.concatenate([own, other], axis=0)
    return lax.all_gather(both, "y", axis=1, tiled=True)


def on_device(
    source_rows,
    short_filters,
    medium_filters,
    skip_gain,
    out_weight,
    doc_lengths,
    block_packing_device,
):
    ny, nx, nz = lax.axis_size("y"), lax.axis_size("x"), lax.axis_size("z")
    stretches = ny * nx
    width = source_rows.shape[2]
    rows = block_packing_device.shape[1] * BLK
    bpd = block_packing_device
    swap = [(0, 1), (1, 0)]

    kv_out, q_out = call(
        pack_kernel,
        [shape((stretches, 2, BLK, width)), shape((stretches, BLK, width))],
        [smem(), vmem()],
        (bpd, source_rows.transpose(1, 0, 2)),
        10**6,
        name="pack",
    )
    kv_in = lax.all_to_all(kv_out, CTX, split_axis=0, concat_axis=0, tiled=True)
    q_in = lax.all_to_all(q_out, CTX, split_axis=0, concat_axis=0, tiled=True)

    weight = weight_columns(out_weight)

    groups = medium_filters.shape[1]
    line = jnp.pad(medium_filters[::-1].T.astype(F32), ((0, 0), (1, HALF - 1)))
    (bands,) = call(
        toeplitz_kernel,
        [shape((groups, HALF, 2 * HALF))],
        [vmem()],
        (line,),
        10**8,
        name="bands",
    )
    bands, kv_in = lax.optimization_barrier((bands, kv_in))

    z, send, head = call(
        z_kernel,
        [shape((rows, width)), shape((HALF + 2 * TAIL, width)), shape((2 * TAIL, width))],
        [smem(), smem(), vmem(), vmem()],
        (bpd, doc_lengths, kv_in, short_filters),
        10**7,
        scratch=[pltpu.VMEM((2, rows + TAIL, width), F32)],
        name="gated",
    )
    recv = passed_along(send)
    (medium,) = call(
        medium_kernel,
        [shape((rows, width), F32)],
        [smem()] + [vmem()] * 6,
        (doc_lengths, z, recv, head, short_filters, bands, skip_gain.reshape(1, width)),
        10**9,
        scratch=[pltpu.VMEM((rows + HALF, width), BF16)],
        name="medium",
    )
    last = lax.dynamic_index_in_dim(bpd, stretch_id(), 0, keepdims=False)[-1]
    q_tail = lax.dynamic_index_in_dim(q_in, last, 0, keepdims=False)[BLK - TAIL :]
    q_halo = passed_along(q_tail)

    pieces = [None, None]
    for half in (1, 0):
        (copies,) = call(
            functools.partial(hidden_kernel, half),
            [shape((nx, HALF, width))],
            [smem(), smem()] + [vmem()] * 4,
            (bpd, doc_lengths, q_in, q_halo if half == 0 else q_tail, short_filters, medium),
            10**7,
            scratch=[pltpu.VMEM((HALF + TAIL, width), F32)],
            name=f"hidden{half}",
        )
        own = lax.all_to_all(copies, "x", split_axis=0, concat_axis=0, tiled=True)
        own = own.reshape(nx * HALF, width)
        other = lax.ppermute(own, "core", swap)
        (partial,) = call(
            project_kernel,
            [shape((nz, nx * HALF, 128))],
            [vmem()] * 3,
            (own, other, weight),
            2 * nx * HALF * 2 * width * nz * 128,
            name=f"project{half}",
        )
        parts = lax.all_to_all(partial, "z", split_axis=0, concat_axis=0, tiled=True)
        total = jnp.sum(parts.astype(F32), axis=0).astype(BF16)
        mine = lax.all_to_all(
            total.reshape(nx, HALF, 128), "x", split_axis=0, concat_axis=0, tiled=True
        )
        pieces[half] = mine
    both = jnp.concatenate(pieces, axis=1)
    return both.transpose(1, 0, 2).reshape(rows, nx * 128)


def solution(mesh):
    ctx, mp = CTX, ("z", "core")
    mesh4 = Mesh(mesh.devices.reshape(SHAPE4), ctx + mp)
    return jax.shard_map(
        on_device,
        mesh=mesh4,
        in_specs=(
            P(ctx, None, mp),
            P(None, None, mp),
            P(None, mp),
            P(mp),
            P(mp, ctx),
            P(),
            P(),
        ),
        out_specs=P(ctx, mp),
        check_vma=False,
    )
```

```python
import jax
import jax.numpy as jnp
from jax import lax
from jax.experimental import pallas as pl
from jax.experimental.pallas import tpu as pltpu
from jax.sharding import Mesh, PartitionSpec as P

CTX = ("y", "x")
SHAPE4 = (8, 4, 8, 2)
BLK = 16
TAIL = 8
HALF = 128
F32, BF16 = jnp.float32, jnp.bfloat16


def smem():
    return pl.BlockSpec(memory_space=pltpu.SMEM)


def vmem():
    return pl.BlockSpec(memory_space=pltpu.VMEM)


def stretch_id():
    return lax.axis_index("y") * lax.axis_size("x") + lax.axis_index("x")


def call(body, outs, ins, args, flops, scratch=(), name=None):
    moved = sum(a.size * a.dtype.itemsize for a in args)
    moved += sum(o.size * o.dtype.itemsize for o in outs)
    return pl.pallas_call(
        body,
        out_shape=outs,
        in_specs=ins,
        out_specs=[vmem()] * len(outs),
        scratch_shapes=list(scratch),
        cost_estimate=pl.CostEstimate(flops=flops, bytes_accessed=moved, transcendentals=0),
        name=name,
    )(*args)


def reach_back(lengths, first, shape):
    at = first + lax.broadcasted_iota(jnp.int32, shape, 0)
    begin = jnp.zeros(shape, jnp.int32)
    start = jnp.int32(0)
    for doc in range(lengths.shape[0]):
        begin = jnp.where(at >= start, start, begin)
        start = start + lengths[doc]
    return at - begin


def short_rows(window, taps_ref, which, back):
    count = back.shape[0]
    total = jnp.zeros(back.shape, F32)
    for step in range(taps_ref.shape[1]):
        tap = taps_ref[which, step : step + 1, :].astype(F32)
        piece = window[TAIL - step : TAIL - step + count]
        total = total + jnp.where(back >= step, tap * piece, 0.0)
    return total


def pack_kernel(bpd, src, kv, q):
    me = stretch_id()

    def one(c, slot):
        mine = jnp.int32(0)
        for k in range(bpd.shape[0]):
            mine = mine | (bpd[k, c] == me).astype(jnp.int32)
        rows = pl.ds(pl.multiple_of(slot * BLK, BLK), BLK)
        kv[c, 0] = src[1, rows, :]
        kv[c, 1] = src[2, rows, :]
        q[c] = src[0, rows, :]
        return slot + mine

    lax.fori_loop(0, bpd.shape[1], one, jnp.int32(0))


def toeplitz_kernel(line, out):
    def one(g, carry):
        row = jnp.broadcast_to(line[pl.ds(g, 1), :], out.shape[1:])
        out[g] = pltpu.roll(row, 0, 1, stride=1, stride_axis=0).astype(BF16)
        return carry

    lax.fori_loop(0, out.shape[0], one, 0)


def z_kernel(bpd, lengths, kv, taps, z, send, head, buf):
    me = stretch_id()
    rows, width = z.shape
    for i in range(2):
        buf[i, 0:TAIL, :] = jnp.zeros((TAIL, width), F32)
    for k in range(rows // BLK):
        s = bpd[k, me]
        for i in range(2):
            buf[i, TAIL + k * BLK : TAIL + (k + 1) * BLK, :] = kv[s, i].astype(F32)

    step = 32

    def chunk(r, carry):
        at = pl.multiple_of(r * step, step)
        back = reach_back(lengths, me * rows + at, (step, width))
        wide = pl.ds(at, step + TAIL)
        keyed = short_rows(buf[0, wide, :], taps, 1, back)
        valued = short_rows(buf[1, wide, :], taps, 2, back)
        z[pl.ds(at, step), :] = (keyed * valued).astype(BF16)
        return carry

    lax.fori_loop(0, rows // step, chunk, 0)
    send[0:HALF, :] = z[rows - HALF :, :]
    for i in range(2):
        send[HALF + i * TAIL : HALF + (i + 1) * TAIL, :] = buf[i, rows : rows + TAIL, :].astype(BF16)
        head[i * TAIL : (i + 1) * TAIL, :] = buf[i, TAIL : 2 * TAIL, :].astype(BF16)


def medium_kernel(lengths, z, recv, head, taps, bands, gain, out, ext):
    me = stretch_id()
    rows, width = z.shape
    back = reach_back(lengths, me * rows, (TAIL, width))
    fixed = []
    for i in range(2):
        tail = recv[HALF + i * TAIL : HALF + (i + 1) * TAIL, :].astype(F32)
        mine = head[i * TAIL : (i + 1) * TAIL, :].astype(F32)
        fixed.append(short_rows(jnp.concatenate([tail, mine], axis=0), taps, 1 + i, back))
    first = (fixed[0] * fixed[1]).astype(BF16).astype(F32)
    ext[0:HALF, :] = recv[0:HALF, :]
    ext[HALF:, :] = z[...]
    later = z[TAIL : 2 * TAIL, :].astype(F32)
    ext[HALF : HALF + 2 * TAIL, :] = jnp.concatenate([first, later], axis=0).astype(BF16)
    lane = 128
    per = lane // (width // bands.shape[0])
    group = lax.broadcasted_iota(jnp.int32, (HALF, lane), 1) // (lane // per)
    for b in range(rows // HALF):
        back = reach_back(lengths, me * rows + b * HALF, (HALF, 2 * HALF))
        i = lax.broadcasted_iota(jnp.int32, (HALF, 2 * HALF), 0)
        p = lax.broadcasted_iota(jnp.int32, (HALF, 2 * HALF), 1)
        keep = jnp.where(i + HALF - p <= back, 1.0, 0.0).astype(BF16)
        for t in range(width // lane):
            cols = slice(t * lane, (t + 1) * lane)
            right = ext[b * HALF : (b + 2) * HALF, cols]
            total = jnp.zeros((HALF, lane), F32)
            for g in range(per):
                got = jnp.dot(bands[t * per + g] * keep, right, preferred_element_type=F32)
                total = jnp.where(group == g, got, total)
            zs = ext[(b + 1) * HALF : (b + 2) * HALF, cols].astype(F32)
            out[b * HALF : (b + 1) * HALF, cols] = total + gain[:, cols] * zs


def hidden_kernel(bpd, lengths, q, halo, taps, medium, out, buf):
    me = stretch_id()
    rows, width = medium.shape
    buf[0:TAIL, :] = halo[...].astype(F32)
    for k in range(rows // BLK):
        buf[TAIL + k * BLK : TAIL + (k + 1) * BLK, :] = q[bpd[k, me]].astype(F32)
    step = 32

    def chunk(r, carry):
        at = pl.multiple_of(r * step, step)
        back = reach_back(lengths, me * rows + at, (step, width))
        query = short_rows(buf[pl.ds(at, step + TAIL), :], taps, 0, back)
        value = (query * medium[pl.ds(at, step), :]).astype(BF16)
        for copy in range(out.shape[0]):
            out[copy, pl.ds(at, step), :] = value
        return carry

    lax.fori_loop(0, rows // step, chunk, 0)


def project_kernel(own, other, weight, out):
    k = own.shape[1]
    lane = out.shape[2]
    for pair in range(out.shape[0] // 2):
        cols = slice(pair * 2 * lane, (pair + 1) * 2 * lane)
        got = jnp.dot(own[...], weight[0:k, cols], preferred_element_type=F32)
        got = got + jnp.dot(other[...], weight[k:, cols], preferred_element_type=F32)
        got = got.astype(BF16)
        out[2 * pair] = got[:, :lane]
        out[2 * pair + 1] = got[:, lane:]


def project(own, other, weight, nx, nz):
    rows = own.shape[0] // nx
    k = own.shape[1]
    cols = weight.shape[1]
    lane = cols // nz
    return pl.pallas_call(
        project_kernel,
        grid=(nx,),
        in_specs=[
            pl.BlockSpec((rows, k), lambda i: (i, 0)),
            pl.BlockSpec((rows, k), lambda i: (i, 0)),
            pl.BlockSpec((2 * k, cols), lambda i: (0, 0)),
        ],
        out_specs=pl.BlockSpec((nz, None, rows, lane), lambda i: (0, i, 0, 0)),
        out_shape=shape((nz, nx, rows, lane)),
        cost_estimate=pl.CostEstimate(
            flops=4 * nx * rows * k * cols, bytes_accessed=8 << 20, transcendentals=0
        ),
        name="project",
    )(own, other, weight)


def sum_kernel(parts, out):
    total = parts[0].astype(F32)
    for i in range(1, parts.shape[0]):
        total = total + parts[i].astype(F32)
    out[...] = total.astype(BF16)


def summed(parts):
    nz, nx, rows, lane = parts.shape
    return pl.pallas_call(
        sum_kernel,
        grid=(nx,),
        in_specs=[pl.BlockSpec((nz, None, rows, lane), lambda i: (0, i, 0, 0))],
        out_specs=pl.BlockSpec((rows, lane), lambda i: (0, i)),
        out_shape=shape((rows, nx * lane)),
        cost_estimate=pl.CostEstimate(
            flops=parts.size, bytes_accessed=2 * parts.size, transcendentals=0
        ),
        name="total",
    )(parts)


def shape(dims, dtype=BF16):
    return jax.ShapeDtypeStruct(dims, dtype)


def passed_along(block):
    n = lax.axis_size(CTX)
    return lax.ppermute(block, CTX, [(i, i + 1) for i in range(n - 1)])


def weight_columns(out_weight):
    nx = lax.axis_size("x")
    core = lax.axis_index("core")
    width = out_weight.shape[1] // 2
    halves = (out_weight[:, :width], out_weight[:, width:])
    same = jnp.where(core == 0, halves[0], halves[1])
    flip = jnp.where(core == 0, halves[1], halves[0])
    route = lambda f: [
        (x * 2 + i, (2 * (x % 2) + f(i)) * 2 + x // 2) for x in range(nx) for i in range(2)
    ]
    a = lax.ppermute(same, ("x", "core"), route(lambda i: i))
    b = lax.ppermute(flip, ("x", "core"), route(lambda i: 1 - i))
    straight = lax.axis_index("x") % 2 == core
    own = jnp.where(straight, a, b)
    other = jnp.where(straight, b, a)
    both = jnp.concatenate([own, other], axis=0)
    return lax.all_gather(both, "y", axis=1, tiled=True)


def on_device(
    source_rows,
    short_filters,
    medium_filters,
    skip_gain,
    out_weight,
    doc_lengths,
    block_packing_device,
):
    ny, nx, nz = lax.axis_size("y"), lax.axis_size("x"), lax.axis_size("z")
    stretches = ny * nx
    width = source_rows.shape[2]
    rows = block_packing_device.shape[1] * BLK
    bpd = block_packing_device.T

    kv_out, q_out = call(
        pack_kernel,
        [shape((stretches, 2, BLK, width)), shape((stretches, BLK, width))],
        [smem(), vmem()],
        (bpd, source_rows.transpose(1, 0, 2)),
        10**6,
        name="pack",
    )
    kv_in = lax.all_to_all(kv_out, CTX, split_axis=0, concat_axis=0, tiled=True)
    q_in = lax.all_to_all(q_out, CTX, split_axis=0, concat_axis=0, tiled=True)

    weight = weight_columns(out_weight)

    groups = medium_filters.shape[1]
    line = jnp.pad(medium_filters[::-1].T.astype(F32), ((0, 0), (1, HALF - 1)))
    (bands,) = call(
        toeplitz_kernel,
        [shape((groups, HALF, 2 * HALF))],
        [vmem()],
        (line,),
        10**8,
        name="bands",
    )
    bands, kv_in = lax.optimization_barrier((bands, kv_in))

    z, send, head = call(
        z_kernel,
        [shape((rows, width)), shape((HALF + 2 * TAIL, width)), shape((2 * TAIL, width))],
        [smem(), smem(), vmem(), vmem()],
        (bpd, doc_lengths, kv_in, short_filters),
        10**7,
        scratch=[pltpu.VMEM((2, rows + TAIL, width), F32)],
        name="gated",
    )
    recv = passed_along(send)
    (medium,) = call(
        medium_kernel,
        [shape((rows, width), F32)],
        [smem()] + [vmem()] * 6,
        (doc_lengths, z, recv, head, short_filters, bands, skip_gain.reshape(1, width)),
        10**9,
        scratch=[pltpu.VMEM((rows + HALF, width), BF16)],
        name="medium",
    )
    medium, q_in = lax.optimization_barrier((medium, q_in))
    last = lax.dynamic_index_in_dim(bpd[-1], stretch_id(), 0, keepdims=False)
    q_tail = lax.dynamic_index_in_dim(q_in, last, 0, keepdims=False)[BLK - TAIL :]
    q_halo = passed_along(q_tail)
    (copies,) = call(
        hidden_kernel,
        [shape((nx, rows, width))],
        [smem(), smem()] + [vmem()] * 4,
        (bpd, doc_lengths, q_in, q_halo, short_filters, medium),
        10**7,
        scratch=[pltpu.VMEM((rows + TAIL, width), F32)],
        name="hidden",
    )
    own = lax.all_to_all(copies, "x", split_axis=0, concat_axis=0, tiled=True)
    own = own.reshape(nx * rows, width)
    other = lax.ppermute(own, "core", [(0, 1), (1, 0)])
    partial = project(own, other, weight, nx, nz)
    flat = partial.reshape(nz * nx, rows, partial.shape[3])
    parts = lax.all_to_all(flat, ("z", "x"), split_axis=0, concat_axis=0, tiled=True)
    return summed(parts.reshape(partial.shape))


def solution(mesh):
    ctx, mp = CTX, ("z", "core")
    mesh4 = Mesh(mesh.devices.reshape(SHAPE4), ctx + mp)
    return jax.shard_map(
        on_device,
        mesh=mesh4,
        in_specs=(
            P(ctx, None, mp),
            P(None, None, mp),
            P(None, mp),
            P(mp),
            P(mp, ctx),
            P(),
            P(),
        ),
        out_specs=P(ctx, mp),
        check_vma=False,
    )
```

```python
import functools

import jax
import jax.numpy as jnp
from jax import lax
from jax.experimental import pallas as pl
from jax.experimental.pallas import tpu as pltpu
from jax.sharding import Mesh, PartitionSpec as P


CTX = ("y", "x")
SHAPE4 = (8, 4, 8, 2)
BLK = 16
TAIL = 8
HALF = 128
F32, BF16 = jnp.float32, jnp.bfloat16


def smem():
    return pl.BlockSpec(memory_space=pltpu.SMEM)


def vmem():
    return pl.BlockSpec(memory_space=pltpu.VMEM)


def stretch_id():
    return lax.axis_index("y") * lax.axis_size("x") + lax.axis_index("x")


def call(body, outs, ins, args, flops, scratch=()):
    moved = sum(a.size * a.dtype.itemsize for a in args)
    moved += sum(o.size * o.dtype.itemsize for o in outs)
    return pl.pallas_call(
        body,
        out_shape=outs,
        in_specs=ins,
        out_specs=[vmem()] * len(outs),
        scratch_shapes=list(scratch),
        cost_estimate=pl.CostEstimate(flops=flops, bytes_accessed=moved, transcendentals=0),
    )(*args)


def reach_back(lengths, first, shape):
    at = first + lax.broadcasted_iota(jnp.int32, shape, 0)
    begin = jnp.zeros(shape, jnp.int32)
    start = jnp.int32(0)
    for doc in range(lengths.shape[0]):
        begin = jnp.where(at >= start, start, begin)
        start = start + lengths[doc]
    return at - begin


def short_rows(window, taps_ref, which, back):
    count = back.shape[0]
    total = jnp.zeros(back.shape, F32)
    for step in range(taps_ref.shape[1]):
        tap = taps_ref[which, step : step + 1, :].astype(F32)
        piece = window[TAIL - step : TAIL - step + count]
        total = total + jnp.where(back >= step, tap * piece, 0.0)
    return total


def pack_kernel(bpd, src, kv, q, slots):
    @pl.when(pl.program_id(0) == 0)
    def _():
        me = stretch_id()

        def count(c, slot):
            mine = bpd[0, c] == me
            for k in range(1, bpd.shape[0]):
                mine = mine | (bpd[k, c] == me)
            slots[c] = slot
            return slot + mine.astype(jnp.int32)

        lax.fori_loop(0, bpd.shape[1], count, jnp.int32(0))

    def one(c, carry):
        rows = pl.ds(pl.multiple_of(slots[c] * BLK, BLK), BLK)
        kv[c, 0] = src[1, rows, :]
        kv[c, 1] = src[2, rows, :]
        q[c] = src[0, rows, :]
        return carry

    lax.fori_loop(0, bpd.shape[1], one, 0, unroll=4)


def packed_blocks(bpd, src, stretches):
    width = src.shape[2]
    lane = width // 4
    return pl.pallas_call(
        pack_kernel,
        grid=(width // lane,),
        in_specs=[smem(), pl.BlockSpec((3, src.shape[1], lane), lambda i: (0, 0, i))],
        out_specs=[
            pl.BlockSpec((stretches, 2, BLK, lane), lambda i: (0, 0, 0, i)),
            pl.BlockSpec((stretches, BLK, lane), lambda i: (0, 0, i)),
        ],
        out_shape=[shape((stretches, 2, BLK, width)), shape((stretches, BLK, width))],
        scratch_shapes=[pltpu.SMEM((stretches,), jnp.int32)],
        cost_estimate=pl.CostEstimate(
            flops=10**6, bytes_accessed=4 * src.size, transcendentals=0
        ),
        name="pack",
    )(bpd, src)


def toeplitz_kernel(line, out):
    def one(g, carry):
        row = jnp.broadcast_to(line[pl.ds(g, 1), :], out.shape[1:])
        out[g] = pltpu.roll(row, 0, 1, stride=1, stride_axis=0).astype(BF16)
        return carry

    lax.fori_loop(0, out.shape[0], one, 0)


def z_kernel(bpd, lengths, kv, taps, z, send, head, buf):
    me = stretch_id()
    rows, width = z.shape
    for i in range(2):
        buf[i, 0:TAIL, :] = jnp.zeros((TAIL, width), F32)
    for k in range(rows // BLK):
        s = bpd[k, me]
        for i in range(2):
            buf[i, TAIL + k * BLK : TAIL + (k + 1) * BLK, :] = kv[s, i].astype(F32)

    step = 32

    def chunk(r, carry):
        at = pl.multiple_of(r * step, step)
        back = reach_back(lengths, me * rows + at, (step, width))
        wide = pl.ds(at, step + TAIL)
        keyed = short_rows(buf[0, wide, :], taps, 1, back)
        valued = short_rows(buf[1, wide, :], taps, 2, back)
        z[pl.ds(at, step), :] = (keyed * valued).astype(BF16)
        return carry

    lax.fori_loop(0, rows // step, chunk, 0)
    send[0:HALF, :] = z[rows - HALF :, :]
    for i in range(2):
        send[HALF + i * TAIL : HALF + (i + 1) * TAIL, :] = buf[i, rows : rows + TAIL, :].astype(BF16)
        head[i * TAIL : (i + 1) * TAIL, :] = buf[i, TAIL : 2 * TAIL, :].astype(BF16)


def medium_kernel(lengths, z, recv, head, taps, bands, gain, out, ext):
    me = stretch_id()
    rows, width = z.shape
    back = reach_back(lengths, me * rows, (TAIL, width))
    fixed = []
    for i in range(2):
        tail = recv[HALF + i * TAIL : HALF + (i + 1) * TAIL, :].astype(F32)
        mine = head[i * TAIL : (i + 1) * TAIL, :].astype(F32)
        fixed.append(short_rows(jnp.concatenate([tail, mine], axis=0), taps, 1 + i, back))
    first = (fixed[0] * fixed[1]).astype(BF16).astype(F32)
    ext[0:HALF, :] = recv[0:HALF, :]
    ext[HALF:, :] = z[...]
    later = z[TAIL : 2 * TAIL, :].astype(F32)
    ext[HALF : HALF + 2 * TAIL, :] = jnp.concatenate([first, later], axis=0).astype(BF16)
    lane = 128
    per = lane // (width // bands.shape[0])
    group = lax.broadcasted_iota(jnp.int32, (HALF, lane), 1) // (lane // per)
    for b in range(rows // HALF):
        back = reach_back(lengths, me * rows + b * HALF, (HALF, 2 * HALF))
        i = lax.broadcasted_iota(jnp.int32, (HALF, 2 * HALF), 0)
        p = lax.broadcasted_iota(jnp.int32, (HALF, 2 * HALF), 1)
        keep = jnp.where(i + HALF - p <= back, 1.0, 0.0).astype(BF16)
        for t in range(width // lane):
            cols = slice(t * lane, (t + 1) * lane)
            right = ext[b * HALF : (b + 2) * HALF, cols]
            total = jnp.zeros((HALF, lane), F32)
            for g in range(per):
                got = jnp.dot(bands[t * per + g] * keep, right, preferred_element_type=F32)
                total = jnp.where(group == g, got, total)
            zs = ext[(b + 1) * HALF : (b + 2) * HALF, cols].astype(F32)
            out[b * HALF : (b + 1) * HALF, cols] = total + gain[:, cols] * zs


def hidden_kernel(bpd, lengths, q, halo, taps, medium, out, buf):
    me = stretch_id()
    rows, width = medium.shape
    buf[0:TAIL, :] = halo[...].astype(F32)
    for k in range(rows // BLK):
        buf[TAIL + k * BLK : TAIL + (k + 1) * BLK, :] = q[bpd[k, me]].astype(F32)
    step = 32

    def chunk(r, carry):
        at = pl.multiple_of(r * step, step)
        back = reach_back(lengths, me * rows + at, (step, width))
        query = short_rows(buf[pl.ds(at, step + TAIL), :], taps, 0, back)
        value = (query * medium[pl.ds(at, step), :]).astype(BF16)
        for copy in range(out.shape[0]):
            out[copy, pl.ds(at, step), :] = value
        return carry

    lax.fori_loop(0, rows // step, chunk, 0)


def project_kernel(offsets, own, other, *refs):
    weights, out = refs[:-1], refs[-1]
    k = own.shape[1]
    lane = out.shape[3]
    n = out.shape[0]
    y = lax.axis_index("y")
    for pair in range(0, n, 2):
        wide = jnp.concatenate([weights[pair][...], weights[pair + 1][...]], axis=1)
        got = jnp.dot(own[...], wide[:k], preferred_element_type=F32)
        got = got + jnp.dot(other[...], wide[k:], preferred_element_type=F32)
        got = got.astype(BF16)
        for i in range(2):
            at = lax.rem(y - offsets[pair + i] + n, n)
            for s in range(out.shape[1]):
                piece = got[s * out.shape[2] : (s + 1) * out.shape[2]]
                out[at, s] = piece[:, i * lane : (i + 1) * lane]


def project(own, other, weights, nx):
    offsets = tuple(w[0] for w in weights)
    blocks = [w[1] for w in weights]
    n = len(blocks)
    rows = own.shape[0] // nx
    two = 2
    k = own.shape[1]
    lane = blocks[0].shape[1]
    return pl.pallas_call(
        functools.partial(project_kernel, offsets),
        grid=(nx // two,),
        in_specs=[
            pl.BlockSpec((two * rows, k), lambda i: (i, 0)),
            pl.BlockSpec((two * rows, k), lambda i: (i, 0)),
        ]
        + [pl.BlockSpec((2 * k, lane), lambda i: (0, 0)) for _ in blocks],
        out_specs=pl.BlockSpec((n, two, rows, lane), lambda i: (0, i, 0, 0)),
        out_shape=shape((n, nx, rows, lane)),
        cost_estimate=pl.CostEstimate(
            flops=4 * nx * rows * k * n * lane, bytes_accessed=8 << 20, transcendentals=0
        ),
        name="project",
    )(own, other, *blocks)


def summed(parts):
    columns = [jnp.sum(parts[:, x].astype(F32), axis=0) for x in range(parts.shape[1])]
    return jnp.concatenate(columns, axis=1).astype(BF16)


def shape(dims, dtype=BF16):
    return jax.ShapeDtypeStruct(dims, dtype)


def passed_along(block):
    n = lax.axis_size(CTX)
    return lax.ppermute(block, CTX, [(i, i + 1) for i in range(n - 1)])


def weight_columns(out_weight):
    nx = lax.axis_size("x")
    core = lax.axis_index("core")
    width = out_weight.shape[1] // 2
    halves = (out_weight[:, :width], out_weight[:, width:])
    same = jnp.where(core == 0, halves[0], halves[1])
    flip = jnp.where(core == 0, halves[1], halves[0])
    route = lambda f: [
        (x * 2 + i, (2 * (x % 2) + f(i)) * 2 + x // 2) for x in range(nx) for i in range(2)
    ]
    a = lax.ppermute(same, ("x", "core"), route(lambda i: i))
    b = lax.ppermute(flip, ("x", "core"), route(lambda i: 1 - i))
    straight = lax.axis_index("x") % 2 == core
    own = jnp.where(straight, a, b)
    other = jnp.where(straight, b, a)
    return jnp.concatenate([own, other], axis=0)


def around(block, distance):
    n = lax.axis_size("y")
    return lax.ppermute(block, "y", [(i, (i + distance) % n) for i in range(n)])


def operator(
    source_rows,
    short_filters,
    medium_filters,
    skip_gain,
    out_weight,
    doc_lengths,
    block_packing_device,
):
    ny, nx, nz = lax.axis_size("y"), lax.axis_size("x"), lax.axis_size("z")
    stretches = ny * nx
    width = source_rows.shape[2]
    rows = block_packing_device.shape[1] * BLK
    bpd = block_packing_device.T

    kv_out, q_out = packed_blocks(bpd, source_rows.transpose(1, 0, 2), stretches)
    kv_in = lax.all_to_all(kv_out, CTX, split_axis=0, concat_axis=0, tiled=True)
    q_in = lax.all_to_all(q_out, CTX, split_axis=0, concat_axis=0, tiled=True)
    block = weight_columns(out_weight)

    groups = medium_filters.shape[1]
    line = jnp.pad(medium_filters[::-1].T.astype(F32), ((0, 0), (1, HALF - 1)))
    (bands,) = call(toeplitz_kernel, [shape((groups, HALF, 2 * HALF))], [vmem()], (line,), 10**8)
    weights = [(0, block)]
    up = down = block
    for d in (1, 2):
        up, down = around(up, 1), around(down, -1)
        weights += [(d, up), (-d, down)]

    z, send, head = call(
        z_kernel,
        [shape((rows, width)), shape((HALF + 2 * TAIL, width)), shape((2 * TAIL, width))],
        [smem(), smem(), vmem(), vmem()],
        (bpd, doc_lengths, kv_in, short_filters),
        10**7,
        scratch=[pltpu.VMEM((2, rows + TAIL, width), F32)],
    )
    recv = passed_along(send)
    (medium,) = call(
        medium_kernel,
        [shape((rows, width), F32)],
        [smem()] + [vmem()] * 6,
        (doc_lengths, z, recv, head, short_filters, bands, skip_gain.reshape(1, width)),
        10**9,
        scratch=[pltpu.VMEM((rows + HALF, width), BF16)],
    )
    medium, q_in = lax.optimization_barrier((medium, q_in))
    up, down = around(up, 1), around(down, -1)
    weights += [(3, up), (-3, down), (4, around(up, 1))]
    mine = jnp.arange(stretches, dtype=jnp.int32) == stretch_id()
    last = jnp.sum(jnp.where(mine, bpd[-1], 0))
    q_tail = lax.dynamic_index_in_dim(q_in, last, 0, keepdims=False)[BLK - TAIL :]
    q_halo = passed_along(q_tail)
    (copies,) = call(
        hidden_kernel,
        [shape((nx, rows, width))],
        [smem(), smem()] + [vmem()] * 4,
        (bpd, doc_lengths, q_in, q_halo, short_filters, medium),
        10**7,
        scratch=[pltpu.VMEM((rows + TAIL, width), F32)],
    )
    own = lax.all_to_all(copies, "x", split_axis=0, concat_axis=0, tiled=True)
    own = own.reshape(nx * rows, width)
    other = lax.ppermute(own, "core", [(0, 1), (1, 0)])
    partial = project(own, other, weights, nx)
    flat = partial.reshape(nz * nx, rows, partial.shape[3])
    parts = lax.all_to_all(flat, ("z", "x"), split_axis=0, concat_axis=0, tiled=True)
    return summed(parts.reshape(partial.shape))


def solution(mesh):
    ctx, mp = CTX, ("z", "core")
    mesh4 = Mesh(mesh.devices.reshape(SHAPE4), ctx + mp)
    return jax.shard_map(
        operator,
        mesh=mesh4,
        in_specs=(
            P(ctx, None, mp),
            P(None, None, mp),
            P(None, mp),
            P(mp),
            P(mp, ctx),
            P(),
            P(),
        ),
        out_specs=P(ctx, mp),
        check_vma=False,
    )
```

```python
import functools

import jax
import jax.numpy as jnp
from jax import lax
from jax.experimental import pallas as pl
from jax.experimental.pallas import tpu as pltpu
from jax.sharding import Mesh, PartitionSpec as P


CTX = ("y", "x")
SHAPE4 = (8, 4, 8, 2)
BLK = 16
TAIL = 8
HALF = 128
F32, BF16 = jnp.float32, jnp.bfloat16


def smem():
    return pl.BlockSpec(memory_space=pltpu.SMEM)


def vmem():
    return pl.BlockSpec(memory_space=pltpu.VMEM)


def stretch_id():
    return lax.axis_index("y") * lax.axis_size("x") + lax.axis_index("x")


def call(body, outs, ins, args, flops, scratch=()):
    moved = sum(a.size * a.dtype.itemsize for a in args)
    moved += sum(o.size * o.dtype.itemsize for o in outs)
    return pl.pallas_call(
        body,
        out_shape=outs,
        in_specs=ins,
        out_specs=[vmem()] * len(outs),
        scratch_shapes=list(scratch),
        cost_estimate=pl.CostEstimate(flops=flops, bytes_accessed=moved, transcendentals=0),
    )(*args)


def reach_back(lengths, first, shape):
    at = first + lax.broadcasted_iota(jnp.int32, shape, 0)
    begin = jnp.zeros(shape, jnp.int32)
    start = jnp.int32(0)
    for doc in range(lengths.shape[0]):
        begin = jnp.where(at >= start, start, begin)
        start = start + lengths[doc]
    return at - begin


def short_rows(window, taps_ref, which, back):
    count = back.shape[0]
    total = jnp.zeros(back.shape, F32)
    for step in range(taps_ref.shape[1]):
        tap = taps_ref[which, step : step + 1, :].astype(F32)
        piece = window[TAIL - step : TAIL - step + count]
        total = total + jnp.where(back >= step, tap * piece, 0.0)
    return total


def pack_kernel(bpd, src, kv, q, sems):
    me = stretch_id()

    def one(c, slot):
        mine = bpd[0, c] == me
        for k in range(1, bpd.shape[0]):
            mine = mine | (bpd[k, c] == me)
        rows = pl.ds(pl.multiple_of(slot * BLK, BLK), BLK)
        pltpu.make_async_copy(src.at[pl.ds(1, 2), rows, :], kv.at[c], sems.at[0]).start()
        pltpu.make_async_copy(src.at[0, rows, :], q.at[c], sems.at[1]).start()
        return slot + mine.astype(jnp.int32)

    lax.fori_loop(0, bpd.shape[1], one, jnp.int32(0), unroll=2)
    pltpu.make_async_copy(kv, kv, sems.at[0]).wait()
    pltpu.make_async_copy(q, q, sems.at[1]).wait()


def packed_blocks(bpd, src, stretches):
    width = src.shape[2]
    return pl.pallas_call(
        pack_kernel,
        in_specs=[smem(), vmem()],
        out_specs=[pl.BlockSpec(memory_space=pl.ANY)] * 2,
        out_shape=[shape((stretches, 2, BLK, width)), shape((stretches, BLK, width))],
        scratch_shapes=[pltpu.SemaphoreType.DMA((2,))],
        cost_estimate=pl.CostEstimate(
            flops=10**6, bytes_accessed=4 * src.size, transcendentals=0
        ),
        name="pack",
    )(bpd, src)


def toeplitz_kernel(line, out):
    def one(g, carry):
        row = jnp.broadcast_to(line[pl.ds(g, 1), :], out.shape[1:])
        out[g] = pltpu.roll(row, 0, 1, stride=1, stride_axis=0).astype(BF16)
        return carry

    lax.fori_loop(0, out.shape[0], one, 0)


def z_kernel(bpd, lengths, kv, taps, z, send, head, buf):
    me = stretch_id()
    rows, width = z.shape
    for i in range(2):
        buf[i, 0:TAIL, :] = jnp.zeros((TAIL, width), F32)
    for k in range(rows // BLK):
        s = bpd[k, me]
        for i in range(2):
            buf[i, TAIL + k * BLK : TAIL + (k + 1) * BLK, :] = kv[s, i].astype(F32)

    step = 32

    def chunk(r, carry):
        at = pl.multiple_of(r * step, step)
        back = reach_back(lengths, me * rows + at, (step, width))
        wide = pl.ds(at, step + TAIL)
        keyed = short_rows(buf[0, wide, :], taps, 1, back)
        valued = short_rows(buf[1, wide, :], taps, 2, back)
        z[pl.ds(at, step), :] = (keyed * valued).astype(BF16)
        return carry

    lax.fori_loop(0, rows // step, chunk, 0)
    send[0:HALF, :] = z[rows - HALF :, :]
    for i in range(2):
        send[HALF + i * TAIL : HALF + (i + 1) * TAIL, :] = buf[i, rows : rows + TAIL, :].astype(BF16)
        head[i * TAIL : (i + 1) * TAIL, :] = buf[i, TAIL : 2 * TAIL, :].astype(BF16)


def medium_kernel(lengths, z, recv, head, taps, bands, gain, out, ext):
    me = stretch_id()
    rows, width = z.shape
    back = reach_back(lengths, me * rows, (TAIL, width))
    fixed = []
    for i in range(2):
        tail = recv[HALF + i * TAIL : HALF + (i + 1) * TAIL, :].astype(F32)
        mine = head[i * TAIL : (i + 1) * TAIL, :].astype(F32)
        fixed.append(short_rows(jnp.concatenate([tail, mine], axis=0), taps, 1 + i, back))
    first = (fixed[0] * fixed[1]).astype(BF16).astype(F32)
    ext[0:HALF, :] = recv[0:HALF, :]
    ext[HALF:, :] = z[...]
    later = z[TAIL : 2 * TAIL, :].astype(F32)
    ext[HALF : HALF + 2 * TAIL, :] = jnp.concatenate([first, later], axis=0).astype(BF16)
    lane = 128
    per = lane // (width // bands.shape[0])
    group = lax.broadcasted_iota(jnp.int32, (HALF, lane), 1) // (lane // per)
    for b in range(rows // HALF):
        back = reach_back(lengths, me * rows + b * HALF, (HALF, 2 * HALF))
        i = lax.broadcasted_iota(jnp.int32, (HALF, 2 * HALF), 0)
        p = lax.broadcasted_iota(jnp.int32, (HALF, 2 * HALF), 1)
        keep = jnp.where(i + HALF - p <= back, 1.0, 0.0).astype(BF16)
        for t in range(width // lane):
            cols = slice(t * lane, (t + 1) * lane)
            right = ext[b * HALF : (b + 2) * HALF, cols]
            total = jnp.zeros((HALF, lane), F32)
            for g in range(per):
                got = jnp.dot(bands[t * per + g] * keep, right, preferred_element_type=F32)
                total = jnp.where(group == g, got, total)
            zs = ext[(b + 1) * HALF : (b + 2) * HALF, cols].astype(F32)
            out[b * HALF : (b + 1) * HALF, cols] = total + gain[:, cols] * zs


def hidden_kernel(bpd, lengths, q, halo, taps, medium, out, buf):
    me = stretch_id()
    rows, width = medium.shape
    buf[0:TAIL, :] = halo[...].astype(F32)
    for k in range(rows // BLK):
        buf[TAIL + k * BLK : TAIL + (k + 1) * BLK, :] = q[bpd[k, me]].astype(F32)
    step = 32

    def chunk(r, carry):
        at = pl.multiple_of(r * step, step)
        back = reach_back(lengths, me * rows + at, (step, width))
        query = short_rows(buf[pl.ds(at, step + TAIL), :], taps, 0, back)
        value = (query * medium[pl.ds(at, step), :]).astype(BF16)
        for copy in range(out.shape[0]):
            out[copy, pl.ds(at, step), :] = value
        return carry

    lax.fori_loop(0, rows // step, chunk, 0)


def project_kernel(offsets, own, other, *refs):
    weights, out = refs[:-1], refs[-1]
    lane = out.shape[3]
    n = out.shape[0]
    y = lax.axis_index("y")
    left = jnp.concatenate([own[...], other[...]], axis=1)
    for pair in range(0, n, 2):
        wide = jnp.concatenate([weights[pair][...], weights[pair + 1][...]], axis=1)
        got = jnp.dot(left, wide, preferred_element_type=F32).astype(BF16)
        for i in range(2):
            at = lax.rem(y - offsets[pair + i] + n, n)
            for s in range(out.shape[1]):
                piece = got[s * out.shape[2] : (s + 1) * out.shape[2]]
                out[at, s] = piece[:, i * lane : (i + 1) * lane]


def project(own, other, weights, nx):
    offsets = tuple(w[0] for w in weights)
    blocks = [w[1] for w in weights]
    n = len(blocks)
    rows = own.shape[0] // nx
    two = 2
    k = own.shape[1]
    lane = blocks[0].shape[1]
    return pl.pallas_call(
        functools.partial(project_kernel, offsets),
        grid=(nx // two,),
        in_specs=[
            pl.BlockSpec((two * rows, k), lambda i: (i, 0)),
            pl.BlockSpec((two * rows, k), lambda i: (i, 0)),
        ]
        + [pl.BlockSpec((2 * k, lane), lambda i: (0, 0)) for _ in blocks],
        out_specs=pl.BlockSpec((n, two, rows, lane), lambda i: (0, i, 0, 0)),
        out_shape=shape((n, nx, rows, lane)),
        cost_estimate=pl.CostEstimate(
            flops=4 * nx * rows * k * n * lane, bytes_accessed=8 << 20, transcendentals=0
        ),
        name="project",
    )(own, other, *blocks)


def summed(parts):
    columns = [jnp.sum(parts[:, x].astype(F32), axis=0) for x in range(parts.shape[1])]
    return jnp.concatenate(columns, axis=1).astype(BF16)


def shape(dims, dtype=BF16):
    return jax.ShapeDtypeStruct(dims, dtype)


def passed_along(block):
    n = lax.axis_size(CTX)
    return lax.ppermute(block, CTX, [(i, i + 1) for i in range(n - 1)])


def weight_columns(out_weight):
    nx = lax.axis_size("x")
    core = lax.axis_index("core")
    width = out_weight.shape[1] // 2
    halves = (out_weight[:, :width], out_weight[:, width:])
    same = jnp.where(core == 0, halves[0], halves[1])
    flip = jnp.where(core == 0, halves[1], halves[0])
    route = lambda f: [
        (x * 2 + i, (2 * (x % 2) + f(i)) * 2 + x // 2) for x in range(nx) for i in range(2)
    ]
    a = lax.ppermute(same, ("x", "core"), route(lambda i: i))
    b = lax.ppermute(flip, ("x", "core"), route(lambda i: 1 - i))
    straight = lax.axis_index("x") % 2 == core
    own = jnp.where(straight, a, b)
    other = jnp.where(straight, b, a)
    return jnp.concatenate([own, other], axis=0)


def around(block, distance):
    n = lax.axis_size("y")
    return lax.ppermute(block, "y", [(i, (i + distance) % n) for i in range(n)])


def operator(
    source_rows,
    short_filters,
    medium_filters,
    skip_gain,
    out_weight,
    doc_lengths,
    block_packing_device,
):
    ny, nx, nz = lax.axis_size("y"), lax.axis_size("x"), lax.axis_size("z")
    stretches = ny * nx
    width = source_rows.shape[2]
    rows = block_packing_device.shape[1] * BLK
    bpd = block_packing_device.T

    kv_out, q_out = packed_blocks(bpd, source_rows.transpose(1, 0, 2), stretches)
    kv_in = lax.all_to_all(kv_out, CTX, split_axis=0, concat_axis=0, tiled=True)
    q_in = lax.all_to_all(q_out, CTX, split_axis=0, concat_axis=0, tiled=True)
    block = weight_columns(out_weight)

    groups = medium_filters.shape[1]
    line = jnp.pad(medium_filters[::-1].T.astype(F32), ((0, 0), (1, HALF - 1)))
    (bands,) = call(toeplitz_kernel, [shape((groups, HALF, 2 * HALF))], [vmem()], (line,), 10**8)
    weights = [(0, block)]
    up = down = block
    for d in (1, 2):
        up, down = around(up, 1), around(down, -1)
        weights += [(d, up), (-d, down)]

    z, send, head = call(
        z_kernel,
        [shape((rows, width)), shape((HALF + 2 * TAIL, width)), shape((2 * TAIL, width))],
        [smem(), smem(), vmem(), vmem()],
        (bpd, doc_lengths, kv_in, short_filters),
        10**7,
        scratch=[pltpu.VMEM((2, rows + TAIL, width), F32)],
    )
    recv = passed_along(send)
    (medium,) = call(
        medium_kernel,
        [shape((rows, width), F32)],
        [smem()] + [vmem()] * 6,
        (doc_lengths, z, recv, head, short_filters, bands, skip_gain.reshape(1, width)),
        10**9,
        scratch=[pltpu.VMEM((rows + HALF, width), BF16)],
    )
    medium, q_in = lax.optimization_barrier((medium, q_in))
    up, down = around(up, 1), around(down, -1)
    weights += [(3, up), (-3, down), (4, around(up, 1))]
    mine = jnp.arange(stretches, dtype=jnp.int32) == stretch_id()
    last = jnp.sum(jnp.where(mine, bpd[-1], 0))
    q_tail = lax.dynamic_index_in_dim(q_in, last, 0, keepdims=False)[BLK - TAIL :]
    q_halo = passed_along(q_tail)
    (copies,) = call(
        hidden_kernel,
        [shape((nx, rows, width))],
        [smem(), smem()] + [vmem()] * 4,
        (bpd, doc_lengths, q_in, q_halo, short_filters, medium),
        10**7,
        scratch=[pltpu.VMEM((rows + TAIL, width), F32)],
    )
    own = lax.all_to_all(copies, "x", split_axis=0, concat_axis=0, tiled=True)
    own = own.reshape(nx * rows, width)
    other = lax.ppermute(own, "core", [(0, 1), (1, 0)])
    partial = project(own, other, weights, nx)
    flat = partial.reshape(nz * nx, rows, partial.shape[3])
    parts = lax.all_to_all(flat, ("z", "x"), split_axis=0, concat_axis=0, tiled=True)
    return summed(parts.reshape(partial.shape))


def solution(mesh):
    ctx, mp = CTX, ("z", "core")
    mesh4 = Mesh(mesh.devices.reshape(SHAPE4), ctx + mp)
    return jax.shard_map(
        operator,
        mesh=mesh4,
        in_specs=(
            P(ctx, None, mp),
            P(None, None, mp),
            P(None, mp),
            P(mp),
            P(mp, ctx),
            P(),
            P(),
        ),
        out_specs=P(ctx, mp),
        check_vma=False,
    )
```

```python
import functools

import jax
import jax.numpy as jnp
from jax import lax
from jax.experimental import pallas as pl
from jax.experimental.pallas import tpu as pltpu
from jax.sharding import Mesh, PartitionSpec as P


CTX = ("y", "x")
SHAPE4 = (8, 4, 8, 2)
BLK = 16
TAIL = 8
HALF = 128
F32, BF16 = jnp.float32, jnp.bfloat16


def smem():
    return pl.BlockSpec(memory_space=pltpu.SMEM)


def vmem():
    return pl.BlockSpec(memory_space=pltpu.VMEM)


def stretch_id():
    return lax.axis_index("y") * lax.axis_size("x") + lax.axis_index("x")


def call(body, outs, ins, args, flops, scratch=()):
    moved = sum(a.size * a.dtype.itemsize for a in args)
    moved += sum(o.size * o.dtype.itemsize for o in outs)
    return pl.pallas_call(
        body,
        out_shape=outs,
        in_specs=ins,
        out_specs=[vmem()] * len(outs),
        scratch_shapes=list(scratch),
        cost_estimate=pl.CostEstimate(flops=flops, bytes_accessed=moved, transcendentals=0),
    )(*args)


def reach_back(lengths, first, shape):
    at = first + lax.broadcasted_iota(jnp.int32, shape, 0)
    begin = jnp.zeros(shape, jnp.int32)
    start = jnp.int32(0)
    for doc in range(lengths.shape[0]):
        begin = jnp.where(at >= start, start, begin)
        start = start + lengths[doc]
    return at - begin


def short_rows(window, taps_ref, which, back):
    count = back.shape[0]
    total = jnp.zeros(back.shape, F32)
    for step in range(taps_ref.shape[1]):
        tap = taps_ref[which, step : step + 1, :].astype(F32)
        piece = window[TAIL - step : TAIL - step + count]
        total = total + jnp.where(back >= step, tap * piece, 0.0)
    return total


def pack_kernel(bpd, src, out, sem):
    me = stretch_id()

    def one(c, slot):
        mine = bpd[0, c] == me
        for k in range(1, bpd.shape[0]):
            mine = mine | (bpd[k, c] == me)
        rows = pl.ds(pl.multiple_of(slot * BLK, BLK), BLK)
        pltpu.make_async_copy(src.at[:, rows, :], out.at[c], sem).start()
        return slot + mine.astype(jnp.int32)

    lax.fori_loop(0, bpd.shape[1], one, jnp.int32(0), unroll=2)
    pltpu.make_async_copy(out, out, sem).wait()


def packed_blocks(bpd, src, stretches):
    return pl.pallas_call(
        pack_kernel,
        in_specs=[smem(), vmem()],
        out_specs=pl.BlockSpec(memory_space=pl.ANY),
        out_shape=shape((stretches, 3, BLK, src.shape[2])),
        scratch_shapes=[pltpu.SemaphoreType.DMA],
        cost_estimate=pl.CostEstimate(
            flops=10**6, bytes_accessed=4 * src.size, transcendentals=0
        ),
        name="pack",
    )(bpd, src)


def toeplitz_kernel(line, out):
    def one(g, carry):
        row = jnp.broadcast_to(line[pl.ds(g, 1), :], out.shape[1:])
        out[g] = pltpu.roll(row, 0, 1, stride=1, stride_axis=0).astype(BF16)
        return carry

    lax.fori_loop(0, out.shape[0], one, 0, unroll=4)


def gather_rows(bpd, blocks, which, buf):
    me = stretch_id()
    buf[0:TAIL, :] = jnp.zeros((TAIL, buf.shape[1]), F32)
    for k in range((buf.shape[0] - TAIL) // BLK):
        buf[TAIL + k * BLK : TAIL + (k + 1) * BLK, :] = blocks[bpd[k, me], which].astype(F32)


STEP = 32


def gated_kernel(bpd, lengths, blocks, taps, z, send, head, buf):
    me = stretch_id()
    rows, width = z.shape
    for i in range(2):
        gather_rows(bpd, blocks, 1 + i, buf.at[i])

    def chunk(r, carry):
        at = pl.multiple_of(r * STEP, STEP)
        back = reach_back(lengths, me * rows + at, (STEP, width))
        wide = pl.ds(at, STEP + TAIL)
        keyed = short_rows(buf[0, wide, :], taps, 1, back)
        valued = short_rows(buf[1, wide, :], taps, 2, back)
        z[pl.ds(at, STEP), :] = (keyed * valued).astype(BF16)
        return carry

    lax.fori_loop(0, rows // STEP, chunk, 0)
    send[0:HALF, :] = z[rows - HALF :, :]
    q_last = blocks[bpd[rows // BLK - 1, me], 0].astype(F32)[BLK - TAIL :]
    q_first = blocks[bpd[0, me], 0].astype(F32)[:TAIL]
    tails = [q_last] + [buf[i, rows : rows + TAIL, :] for i in range(2)]
    heads = [q_first] + [buf[i, TAIL : 2 * TAIL, :] for i in range(2)]
    for i in range(3):
        send[HALF + i * TAIL : HALF + (i + 1) * TAIL, :] = tails[i].astype(BF16)
        head[i * TAIL : (i + 1) * TAIL, :] = heads[i].astype(BF16)


def query_kernel(bpd, lengths, blocks, taps, out, buf):
    me = stretch_id()
    rows, width = out.shape
    gather_rows(bpd, blocks, 0, buf)

    def chunk(r, carry):
        at = pl.multiple_of(r * STEP, STEP)
        back = reach_back(lengths, me * rows + at, (STEP, width))
        out[pl.ds(at, STEP), :] = short_rows(buf[pl.ds(at, STEP + TAIL), :], taps, 0, back)
        return carry

    lax.fori_loop(0, rows // STEP, chunk, 0)


def hidden_kernel(lengths, z, query, recv, head, taps, bands, gain, out, ext, first_q):
    me = stretch_id()
    rows, width = z.shape
    back = reach_back(lengths, me * rows, (TAIL, width))
    fixed = []
    for i in range(3):
        tail = recv[HALF + i * TAIL : HALF + (i + 1) * TAIL, :].astype(F32)
        mine = head[i * TAIL : (i + 1) * TAIL, :].astype(F32)
        fixed.append(short_rows(jnp.concatenate([tail, mine], axis=0), taps, i, back))
    first = (fixed[1] * fixed[2]).astype(BF16).astype(F32)
    ext[0:HALF, :] = recv[0:HALF, :]
    ext[HALF:, :] = z[...]
    later = z[TAIL : 2 * TAIL, :].astype(F32)
    ext[HALF : HALF + 2 * TAIL, :] = jnp.concatenate([first, later], axis=0).astype(BF16)
    first_q[0:TAIL, :] = fixed[0]
    first_q[TAIL:, :] = query[TAIL:HALF, :]
    lane = 128
    per = lane // (width // bands.shape[0])
    group = lax.broadcasted_iota(jnp.int32, (HALF, lane), 1) // (lane // per)
    for b in range(rows // HALF):
        back = reach_back(lengths, me * rows + b * HALF, (HALF, 2 * HALF))
        i = lax.broadcasted_iota(jnp.int32, (HALF, 2 * HALF), 0)
        p = lax.broadcasted_iota(jnp.int32, (HALF, 2 * HALF), 1)
        keep = jnp.where(i + HALF - p <= back, 1.0, 0.0).astype(BF16)
        for t in range(width // lane):
            cols = slice(t * lane, (t + 1) * lane)
            right = ext[b * HALF : (b + 2) * HALF, cols]
            total = jnp.zeros((HALF, lane), F32)
            for g in range(per):
                got = jnp.dot(bands[t * per + g] * keep, right, preferred_element_type=F32)
                total = jnp.where(group == g, got, total)
            zs = ext[(b + 1) * HALF : (b + 2) * HALF, cols].astype(F32)
            q = first_q[:, cols] if b == 0 else query[b * HALF : (b + 1) * HALF, cols]
            value = (q * (total + gain[:, cols] * zs)).astype(BF16)
            for copy in range(out.shape[0]):
                out[copy, b * HALF : (b + 1) * HALF, cols] = value


def relay_kernel(up, down, up_out, down_out):
    up_out[...] = up[...]
    down_out[...] = down[...]


def project_kernel(offsets, own, other, *refs):
    weights, out = refs[:-1], refs[-1]
    lane = out.shape[3]
    n = out.shape[0]
    y = lax.axis_index("y")
    left = jnp.concatenate([own[...], other[...]], axis=1)
    for pair in range(0, n, 2):
        wide = jnp.concatenate([weights[pair][...], weights[pair + 1][...]], axis=1)
        got = jnp.dot(left, wide, preferred_element_type=F32).astype(BF16)
        for i in range(2):
            at = lax.rem(y - offsets[pair + i] + n, n)
            for s in range(out.shape[1]):
                piece = got[s * out.shape[2] : (s + 1) * out.shape[2]]
                out[at, s] = piece[:, i * lane : (i + 1) * lane]


def project(own, other, weights, nx):
    offsets = tuple(w[0] for w in weights)
    blocks = [w[1] for w in weights]
    n = len(blocks)
    rows = own.shape[0] // nx
    two = 2
    k = own.shape[1]
    lane = blocks[0].shape[1]
    return pl.pallas_call(
        functools.partial(project_kernel, offsets),
        grid=(nx // two,),
        in_specs=[
            pl.BlockSpec((two * rows, k), lambda i: (i, 0)),
            pl.BlockSpec((two * rows, k), lambda i: (i, 0)),
        ]
        + [pl.BlockSpec((2 * k, lane), lambda i: (0, 0)) for _ in blocks],
        out_specs=pl.BlockSpec((n, two, rows, lane), lambda i: (0, i, 0, 0)),
        out_shape=shape((n, nx, rows, lane)),
        cost_estimate=pl.CostEstimate(
            flops=4 * nx * rows * k * n * lane, bytes_accessed=8 << 20, transcendentals=0
        ),
        name="project",
    )(own, other, *blocks)


def summed(parts):
    columns = [jnp.sum(parts[:, x].astype(F32), axis=0) for x in range(parts.shape[1])]
    return jnp.concatenate(columns, axis=1).astype(BF16)


def shape(dims, dtype=BF16):
    return jax.ShapeDtypeStruct(dims, dtype)


def passed_along(block):
    n = lax.axis_size(CTX)
    return lax.ppermute(block, CTX, [(i, i + 1) for i in range(n - 1)])


def weight_columns(out_weight):
    nx = lax.axis_size("x")
    core = lax.axis_index("core")
    width = out_weight.shape[1] // 2
    halves = (out_weight[:, :width], out_weight[:, width:])
    same = jnp.where(core == 0, halves[0], halves[1])
    flip = jnp.where(core == 0, halves[1], halves[0])
    route = lambda f: [
        (x * 2 + i, (2 * (x % 2) + f(i)) * 2 + x // 2) for x in range(nx) for i in range(2)
    ]
    a = lax.ppermute(same, ("x", "core"), route(lambda i: i))
    b = lax.ppermute(flip, ("x", "core"), route(lambda i: 1 - i))
    straight = lax.axis_index("x") % 2 == core
    own = jnp.where(straight, a, b)
    other = jnp.where(straight, b, a)
    return jnp.concatenate([own, other], axis=0)


def around(block, distance):
    n = lax.axis_size("y")
    return lax.ppermute(block, "y", [(i, (i + distance) % n) for i in range(n)])


def operator(
    source_rows,
    short_filters,
    medium_filters,
    skip_gain,
    out_weight,
    doc_lengths,
    block_packing_device,
):
    ny, nx, nz = lax.axis_size("y"), lax.axis_size("x"), lax.axis_size("z")
    stretches = ny * nx
    width = source_rows.shape[2]
    rows = block_packing_device.shape[1] * BLK
    bpd = block_packing_device.T

    packed = packed_blocks(bpd, source_rows.transpose(1, 0, 2), stretches)
    blocks = lax.all_to_all(packed, CTX, split_axis=0, concat_axis=0, tiled=True)

    block = weight_columns(out_weight)
    weights = [(0, block)]
    up = down = block
    for d in (1, 2, 3, 4):
        up = around(up, 1)
        down = around(down, -1) if d < 4 else None
        if d == 3:
            both = [shape(up.shape)] * 2
            up, down = call(relay_kernel, both, [vmem()] * 2, (up, down), 0)
        weights += [(d, up)] if down is None else [(d, up), (-d, down)]

    groups = medium_filters.shape[1]
    line = jnp.pad(medium_filters[::-1].T.astype(F32), ((0, 0), (1, HALF - 1)))
    (bands,) = call(toeplitz_kernel, [shape((groups, HALF, 2 * HALF))], [vmem()], (line,), 10**8)

    z, send, head = call(
        gated_kernel,
        [shape((rows, width)), shape((HALF + 3 * TAIL, width)), shape((3 * TAIL, width))],
        [smem(), smem(), vmem(), vmem()],
        (bpd, doc_lengths, blocks, short_filters),
        10**7,
        scratch=[pltpu.VMEM((2, rows + TAIL, width), F32)],
    )
    recv = passed_along(send)
    (query,) = call(
        query_kernel,
        [shape((rows, width), F32)],
        [smem(), smem(), vmem(), vmem()],
        (bpd, doc_lengths, blocks, short_filters),
        10**7,
        scratch=[pltpu.VMEM((rows + TAIL, width), F32)],
    )
    gain = skip_gain.reshape(1, width)
    (copies,) = call(
        hidden_kernel,
        [shape((nx, rows, width))],
        [smem()] + [vmem()] * 7,
        (doc_lengths, z, query, recv, head, short_filters, bands, gain),
        10**9,
        scratch=[pltpu.VMEM((rows + HALF, width), BF16), pltpu.VMEM((HALF, width), F32)],
    )
    own = lax.all_to_all(copies, "x", split_axis=0, concat_axis=0, tiled=True)
    own = own.reshape(nx * rows, width)
    other = lax.ppermute(own, "core", [(0, 1), (1, 0)])
    partial = project(own, other, weights, nx)
    flat = partial.reshape(nz * nx, rows, partial.shape[3])
    parts = lax.all_to_all(flat, ("z", "x"), split_axis=0, concat_axis=0, tiled=True)
    return summed(parts.reshape(partial.shape))


def solution(mesh):
    ctx, mp = CTX, ("z", "core")
    mesh4 = Mesh(mesh.devices.reshape(SHAPE4), ctx + mp)
    return jax.shard_map(
        operator,
        mesh=mesh4,
        in_specs=(
            P(ctx, None, mp),
            P(None, None, mp),
            P(None, mp),
            P(mp),
            P(mp, ctx),
            P(),
            P(),
        ),
        out_specs=P(ctx, mp),
        check_vma=False,
    )
```

```python
import functools

import jax
import jax.numpy as jnp
from jax import lax
from jax.experimental import pallas as pl
from jax.experimental.pallas import tpu as pltpu
from jax.sharding import Mesh, PartitionSpec as P


CTX = ("y", "x")
SHAPE5 = (8, 4, 4, 2, 2)
BLK = 16
TAIL = 8
GRANT = 24 << 20
HALF = 128
F32, BF16 = jnp.float32, jnp.bfloat16


def smem():
    return pl.BlockSpec(memory_space=pltpu.SMEM)


def vmem():
    return pl.BlockSpec(memory_space=pltpu.VMEM)


def stretch_id():
    return lax.axis_index("y") * lax.axis_size("x") + lax.axis_index("x")


def call(body, outs, ins, args, flops, scratch=()):
    moved = sum(a.size * a.dtype.itemsize for a in args)
    moved += sum(o.size * o.dtype.itemsize for o in outs)
    return pl.pallas_call(
        body,
        out_shape=outs,
        in_specs=ins,
        out_specs=[vmem()] * len(outs),
        scratch_shapes=list(scratch),
        compiler_params=pltpu.CompilerParams(vmem_limit_bytes=GRANT),
        cost_estimate=pl.CostEstimate(flops=flops, bytes_accessed=moved, transcendentals=0),
    )(*args)


def reach_back(lengths, first, shape):
    at = first + lax.broadcasted_iota(jnp.int32, shape, 0)
    begin = jnp.zeros(shape, jnp.int32)
    start = jnp.int32(0)
    for doc in range(lengths.shape[0]):
        begin = jnp.where(at >= start, start, begin)
        start = start + lengths[doc]
    return at - begin


def short_rows(window, taps_ref, which, back):
    count = back.shape[0]
    total = jnp.zeros(back.shape, F32)
    for step in range(taps_ref.shape[1]):
        tap = taps_ref[which, step : step + 1, :].astype(F32)
        piece = window[TAIL - step : TAIL - step + count]
        total = total + jnp.where(back >= step, tap * piece, 0.0)
    return total


def pack_kernel(bpd, src, out, sem):
    me = stretch_id()

    def one(c, slot):
        mine = bpd[0, c] == me
        for k in range(1, bpd.shape[0]):
            mine = mine | (bpd[k, c] == me)
        rows = pl.ds(pl.multiple_of(slot * BLK, BLK), BLK)
        pltpu.make_async_copy(src.at[:, rows, :], out.at[c], sem).start()
        return slot + mine.astype(jnp.int32)

    lax.fori_loop(0, bpd.shape[1], one, jnp.int32(0), unroll=2)
    pltpu.make_async_copy(out, out, sem).wait()


def packed_blocks(bpd, src, stretches):
    return pl.pallas_call(
        pack_kernel,
        in_specs=[smem(), vmem()],
        out_specs=pl.BlockSpec(memory_space=pl.ANY),
        out_shape=shape((stretches, 3, BLK, src.shape[2])),
        scratch_shapes=[pltpu.SemaphoreType.DMA],
        cost_estimate=pl.CostEstimate(
            flops=10**6, bytes_accessed=4 * src.size, transcendentals=0
        ),
        compiler_params=pltpu.CompilerParams(vmem_limit_bytes=GRANT),
        name="pack",
    )(bpd, src)


def toeplitz_kernel(line, out):
    def one(g, carry):
        row = jnp.broadcast_to(line[pl.ds(g, 1), :], out.shape[1:])
        out[g] = pltpu.roll(row, 0, 1, stride=1, stride_axis=0).astype(BF16)
        return carry

    lax.fori_loop(0, out.shape[0], one, 0, unroll=4)


def gather_rows(bpd, blocks, which, buf):
    me = stretch_id()
    buf[0:TAIL, :] = jnp.zeros((TAIL, buf.shape[1]), F32)
    for k in range((buf.shape[0] - TAIL) // BLK):
        buf[TAIL + k * BLK : TAIL + (k + 1) * BLK, :] = blocks[bpd[k, me], which].astype(F32)


STEP = 32


def gated_kernel(bpd, lengths, blocks, taps, z, send, head, buf):
    me = stretch_id()
    rows, width = z.shape
    for i in range(2):
        gather_rows(bpd, blocks, 1 + i, buf.at[i])

    def chunk(r, carry):
        at = pl.multiple_of(r * STEP, STEP)
        back = reach_back(lengths, me * rows + at, (STEP, width))
        wide = pl.ds(at, STEP + TAIL)
        keyed = short_rows(buf[0, wide, :], taps, 1, back)
        valued = short_rows(buf[1, wide, :], taps, 2, back)
        z[pl.ds(at, STEP), :] = (keyed * valued).astype(BF16)
        return carry

    lax.fori_loop(0, rows // STEP, chunk, 0)
    send[0:HALF, :] = z[rows - HALF :, :]
    q_last = blocks[bpd[rows // BLK - 1, me], 0].astype(F32)[BLK - TAIL :]
    q_first = blocks[bpd[0, me], 0].astype(F32)[:TAIL]
    tails = [q_last] + [buf[i, rows : rows + TAIL, :] for i in range(2)]
    heads = [q_first] + [buf[i, TAIL : 2 * TAIL, :] for i in range(2)]
    for i in range(3):
        send[HALF + i * TAIL : HALF + (i + 1) * TAIL, :] = tails[i].astype(BF16)
        head[i * TAIL : (i + 1) * TAIL, :] = heads[i].astype(BF16)


def query_kernel(bpd, lengths, blocks, taps, out, buf):
    me = stretch_id()
    rows, width = out.shape
    gather_rows(bpd, blocks, 0, buf)

    def chunk(r, carry):
        at = pl.multiple_of(r * STEP, STEP)
        back = reach_back(lengths, me * rows + at, (STEP, width))
        out[pl.ds(at, STEP), :] = short_rows(buf[pl.ds(at, STEP + TAIL), :], taps, 0, back)
        return carry

    lax.fori_loop(0, rows // STEP, chunk, 0)


def hidden_kernel(lengths, z, query, recv, head, taps, bands, gain, out, ext, first_q):
    me = stretch_id()
    rows, width = z.shape
    back = reach_back(lengths, me * rows, (TAIL, width))
    fixed = []
    for i in range(3):
        tail = recv[HALF + i * TAIL : HALF + (i + 1) * TAIL, :].astype(F32)
        mine = head[i * TAIL : (i + 1) * TAIL, :].astype(F32)
        fixed.append(short_rows(jnp.concatenate([tail, mine], axis=0), taps, i, back))
    first = (fixed[1] * fixed[2]).astype(BF16).astype(F32)
    ext[0:HALF, :] = recv[0:HALF, :]
    ext[HALF:, :] = z[...]
    later = z[TAIL : 2 * TAIL, :].astype(F32)
    ext[HALF : HALF + 2 * TAIL, :] = jnp.concatenate([first, later], axis=0).astype(BF16)
    first_q[0:TAIL, :] = fixed[0]
    first_q[TAIL:, :] = query[TAIL:HALF, :]
    lane = 128
    per = lane // (width // bands.shape[0])
    group = lax.broadcasted_iota(jnp.int32, (HALF, lane), 1) // (lane // per)
    for b in range(rows // HALF):
        back = reach_back(lengths, me * rows + b * HALF, (HALF, 2 * HALF))
        i = lax.broadcasted_iota(jnp.int32, (HALF, 2 * HALF), 0)
        p = lax.broadcasted_iota(jnp.int32, (HALF, 2 * HALF), 1)
        keep = jnp.where(i + HALF - p <= back, 1.0, 0.0).astype(BF16)
        for t in range(width // lane):
            cols = slice(t * lane, (t + 1) * lane)
            right = ext[b * HALF : (b + 2) * HALF, cols]
            total = jnp.zeros((HALF, lane), F32)
            for g in range(per):
                got = jnp.dot(bands[t * per + g] * keep, right, preferred_element_type=F32)
                total = jnp.where(group == g, got, total)
            zs = ext[(b + 1) * HALF : (b + 2) * HALF, cols].astype(F32)
            q = first_q[:, cols] if b == 0 else query[b * HALF : (b + 1) * HALF, cols]
            value = (q * (total + gain[:, cols] * zs)).astype(BF16)
            for copy in range(out.shape[0]):
                out[copy, b * HALF : (b + 1) * HALF, cols] = value


def relay_kernel(up, down, up_out, down_out):
    up_out[...] = up[...]
    down_out[...] = down[...]


def project_kernel(offsets, part, own, other, *refs):
    weights, (same, cross) = refs[:-2], refs[-2:]
    count, rows, lane = same.shape[1:]
    n = len(weights)
    y = lax.axis_index("y")
    at = slice(part * count * rows, (part + 1) * count * rows)
    left = jnp.concatenate([own[at, :], other[at, :]], axis=1)
    for pair in range(0, n, 2):
        wide = jnp.concatenate([weights[pair][...], weights[pair + 1][...]], axis=1)
        got = jnp.dot(left, wide, preferred_element_type=F32).astype(BF16)
        for i in range(2):
            owner = lax.rem(y - offsets[pair + i] + n, n)
            high = lax.div(owner, 2)
            odd = lax.rem(owner + lax.axis_index("zl"), 2)
            piece = got[:, i * lane : (i + 1) * lane].reshape(count, rows, lane)

            @pl.when(odd == 0)
            def _():
                same[high] = piece

            @pl.when(odd == 1)
            def _():
                cross[high] = piece


def project(part, own, other, weights, nx):
    rows = own.shape[0] // nx
    blocks = [w[1] for w in weights]
    lane = blocks[0].shape[1]
    return call(
        functools.partial(project_kernel, tuple(w[0] for w in weights), part),
        [shape((len(blocks) // 2, nx // 2, rows, lane))] * 2,
        [vmem()] * (2 + len(blocks)),
        (own, other, *blocks),
        2 * own.size * len(blocks) * lane,
    )


def pair_kernel(own0, own1, got0, got1, out):
    count = own0.shape[1]

    def one(z, carry):
        for i, (own, got) in enumerate(((own0, got0), (own1, got1))):
            for s in range(count):
                total = own[z, s].astype(F32) + got[z, s].astype(F32)
                out[z, i * count + s] = total.astype(BF16)
        return carry

    lax.fori_loop(0, own0.shape[0], one, 0)


def along_z(block, distance):
    n = lax.axis_size(("zh", "zl"))
    return lax.ppermute(block, ("zh", "zl"), [(i, (i + distance) % n) for i in range(n)])


def summed(parts):
    columns = [jnp.sum(parts[:, x].astype(F32), axis=0) for x in range(parts.shape[1])]
    return jnp.concatenate(columns, axis=1).astype(BF16)


def shape(dims, dtype=BF16):
    return jax.ShapeDtypeStruct(dims, dtype)


def passed_along(block):
    n = lax.axis_size(CTX)
    return lax.ppermute(block, CTX, [(i, i + 1) for i in range(n - 1)])


def weight_columns(out_weight):
    nx = lax.axis_size("x")
    core = lax.axis_index("core")
    width = out_weight.shape[1] // 2
    halves = (out_weight[:, :width], out_weight[:, width:])
    same = jnp.where(core == 0, halves[0], halves[1])
    flip = jnp.where(core == 0, halves[1], halves[0])
    route = lambda f: [
        (x * 2 + i, (2 * (x % 2) + f(i)) * 2 + x // 2) for x in range(nx) for i in range(2)
    ]
    a = lax.ppermute(same, ("x", "core"), route(lambda i: i))
    b = lax.ppermute(flip, ("x", "core"), route(lambda i: 1 - i))
    straight = lax.axis_index("x") % 2 == core
    own = jnp.where(straight, a, b)
    other = jnp.where(straight, b, a)
    return jnp.concatenate([own, other], axis=0)


def around(block, distance):
    n = lax.axis_size("y")
    return lax.ppermute(block, "y", [(i, (i + distance) % n) for i in range(n)])


def operator(
    source_rows,
    short_filters,
    medium_filters,
    skip_gain,
    out_weight,
    doc_lengths,
    block_packing_device,
):
    ny, nx = lax.axis_size("y"), lax.axis_size("x")
    stretches = ny * nx
    width = source_rows.shape[2]
    rows = block_packing_device.shape[1] * BLK
    bpd = block_packing_device.T

    packed = packed_blocks(bpd, source_rows.transpose(1, 0, 2), stretches)
    blocks = lax.all_to_all(packed, CTX, split_axis=0, concat_axis=0, tiled=True)

    block = weight_columns(out_weight)
    weights = [(0, block)]
    up = down = block
    for d in (1, 2, 3, 4):
        up = around(up, 1)
        down = around(down, -1) if d < 4 else None
        if d == 3:
            both = [shape(up.shape)] * 2
            up, down = call(relay_kernel, both, [vmem()] * 2, (up, down), 0)
        weights += [(d, up)] if down is None else [(d, up), (-d, down)]

    groups = medium_filters.shape[1]
    line = jnp.pad(medium_filters[::-1].T.astype(F32), ((0, 0), (1, HALF - 1)))
    (bands,) = call(toeplitz_kernel, [shape((groups, HALF, 2 * HALF))], [vmem()], (line,), 10**8)

    z, send, head = call(
        gated_kernel,
        [shape((rows, width)), shape((HALF + 3 * TAIL, width)), shape((3 * TAIL, width))],
        [smem(), smem(), vmem(), vmem()],
        (bpd, doc_lengths, blocks, short_filters),
        10**7,
        scratch=[pltpu.VMEM((2, rows + TAIL, width), F32)],
    )
    recv = passed_along(send)
    (query,) = call(
        query_kernel,
        [shape((rows, width), F32)],
        [smem(), smem(), vmem(), vmem()],
        (bpd, doc_lengths, blocks, short_filters),
        10**7,
        scratch=[pltpu.VMEM((rows + TAIL, width), F32)],
    )
    gain = skip_gain.reshape(1, width)
    (copies,) = call(
        hidden_kernel,
        [shape((nx, rows, width))],
        [smem()] + [vmem()] * 7,
        (doc_lengths, z, query, recv, head, short_filters, bands, gain),
        10**9,
        scratch=[pltpu.VMEM((rows + HALF, width), BF16), pltpu.VMEM((HALF, width), F32)],
    )
    own = lax.all_to_all(copies, "x", split_axis=0, concat_axis=0, tiled=True)
    own = own.reshape(nx * rows, width)
    other = lax.ppermute(own, "core", [(0, 1), (1, 0)])
    mine, got = [], []
    for part, distance in ((0, 1), (1, -1)):
        same, cross = project(part, own, other, weights, nx)
        mine.append(same)
        got.append(along_z(cross, distance))
    nzh, _, _, lane = mine[0].shape
    (pairs,) = call(pair_kernel, [shape((nzh, nx, rows, lane))], [vmem()] * 4, (*mine, *got), 10**6)
    flat = pairs.reshape(nzh * nx, rows, lane)
    parts = lax.all_to_all(flat, ("zh", "x"), split_axis=0, concat_axis=0, tiled=True)
    return summed(parts.reshape(pairs.shape))


def solution(mesh):
    ctx, mp = CTX, ("zh", "zl", "core")
    mesh5 = Mesh(mesh.devices.reshape(SHAPE5), ctx + mp)
    return jax.shard_map(
        operator,
        mesh=mesh5,
        in_specs=(
            P(ctx, None, mp),
            P(None, None, mp),
            P(None, mp),
            P(mp),
            P(mp, ctx),
            P(),
            P(),
        ),
        out_specs=P(ctx, mp),
        check_vma=False,
    )
```

```python
import functools

import jax
import jax.numpy as jnp
from jax import lax
from jax.experimental import pallas as pl
from jax.experimental.pallas import tpu as pltpu
from jax.sharding import Mesh, PartitionSpec as P


CTX = ("y", "x")
SHAPE5 = (8, 4, 4, 2, 2)
BLK = 16
TAIL = 8
GRANT = 24 << 20
HALF = 128
F32, BF16 = jnp.float32, jnp.bfloat16


def smem():
    return pl.BlockSpec(memory_space=pltpu.SMEM)


def vmem():
    return pl.BlockSpec(memory_space=pltpu.VMEM)


def stretch_id():
    return lax.axis_index("y") * lax.axis_size("x") + lax.axis_index("x")


def call(body, outs, ins, args, flops, scratch=()):
    moved = sum(a.size * a.dtype.itemsize for a in args)
    moved += sum(o.size * o.dtype.itemsize for o in outs)
    return pl.pallas_call(
        body,
        out_shape=outs,
        in_specs=ins,
        out_specs=[vmem()] * len(outs),
        scratch_shapes=list(scratch),
        compiler_params=pltpu.CompilerParams(vmem_limit_bytes=GRANT),
        cost_estimate=pl.CostEstimate(flops=flops, bytes_accessed=moved, transcendentals=0),
    )(*args)


def reach_back(lengths, first, shape):
    at = first + lax.broadcasted_iota(jnp.int32, shape, 0)
    begin = jnp.zeros(shape, jnp.int32)
    start = jnp.int32(0)
    for doc in range(lengths.shape[0]):
        begin = jnp.where(at >= start, start, begin)
        start = start + lengths[doc]
    return at - begin


def short_rows(window, taps_ref, which, back):
    count = back.shape[0]
    total = jnp.zeros(back.shape, F32)
    for step in range(taps_ref.shape[1]):
        tap = taps_ref[which, step : step + 1, :].astype(F32)
        piece = window[TAIL - step : TAIL - step + count]
        total = total + jnp.where(back >= step, tap * piece, 0.0)
    return total


def pack_kernel(bpd, src, out, sem):
    me = stretch_id()

    def one(c, slot):
        mine = bpd[0, c] == me
        for k in range(1, bpd.shape[0]):
            mine = mine | (bpd[k, c] == me)
        rows = pl.ds(pl.multiple_of(slot * BLK, BLK), BLK)
        pltpu.make_async_copy(src.at[:, rows, :], out.at[c], sem).start()
        return slot + mine.astype(jnp.int32)

    lax.fori_loop(0, bpd.shape[1], one, jnp.int32(0), unroll=2)
    pltpu.make_async_copy(out, out, sem).wait()


def packed_blocks(bpd, src, stretches):
    return pl.pallas_call(
        pack_kernel,
        in_specs=[smem(), vmem()],
        out_specs=pl.BlockSpec(memory_space=pl.ANY),
        out_shape=shape((stretches, 3, BLK, src.shape[2])),
        scratch_shapes=[pltpu.SemaphoreType.DMA],
        cost_estimate=pl.CostEstimate(
            flops=10**6, bytes_accessed=4 * src.size, transcendentals=0
        ),
        compiler_params=pltpu.CompilerParams(vmem_limit_bytes=GRANT),
        name="pack",
    )(bpd, src)


def toeplitz_kernel(line, out):
    def one(g, carry):
        row = jnp.broadcast_to(line[pl.ds(g, 1), :], out.shape[1:])
        out[g] = pltpu.roll(row, 0, 1, stride=1, stride_axis=0).astype(BF16)
        return carry

    lax.fori_loop(0, out.shape[0], one, 0, unroll=4)


def gather_rows(bpd, blocks, which, buf):
    me = stretch_id()
    buf[0:TAIL, :] = jnp.zeros((TAIL, buf.shape[1]), F32)
    for k in range((buf.shape[0] - TAIL) // BLK):
        buf[TAIL + k * BLK : TAIL + (k + 1) * BLK, :] = blocks[bpd[k, me], which].astype(F32)


STEP = 32


def gated_kernel(bpd, lengths, blocks, taps, z, send, head, buf):
    me = stretch_id()
    rows, width = z.shape
    for i in range(2):
        gather_rows(bpd, blocks, 1 + i, buf.at[i])

    def chunk(r, carry):
        at = pl.multiple_of(r * STEP, STEP)
        back = reach_back(lengths, me * rows + at, (STEP, width))
        wide = pl.ds(at, STEP + TAIL)
        keyed = short_rows(buf[0, wide, :], taps, 1, back)
        valued = short_rows(buf[1, wide, :], taps, 2, back)
        z[pl.ds(at, STEP), :] = (keyed * valued).astype(BF16)
        return carry

    lax.fori_loop(0, rows // STEP, chunk, 0)
    send[0:HALF, :] = z[rows - HALF :, :]
    q_last = blocks[bpd[rows // BLK - 1, me], 0].astype(F32)[BLK - TAIL :]
    q_first = blocks[bpd[0, me], 0].astype(F32)[:TAIL]
    tails = [q_last] + [buf[i, rows : rows + TAIL, :] for i in range(2)]
    heads = [q_first] + [buf[i, TAIL : 2 * TAIL, :] for i in range(2)]
    for i in range(3):
        send[HALF + i * TAIL : HALF + (i + 1) * TAIL, :] = tails[i].astype(BF16)
        head[i * TAIL : (i + 1) * TAIL, :] = heads[i].astype(BF16)


def query_kernel(bpd, lengths, blocks, taps, out, buf):
    me = stretch_id()
    rows, width = out.shape
    gather_rows(bpd, blocks, 0, buf)

    def chunk(r, carry):
        at = pl.multiple_of(r * STEP, STEP)
        back = reach_back(lengths, me * rows + at, (STEP, width))
        out[pl.ds(at, STEP), :] = short_rows(buf[pl.ds(at, STEP + TAIL), :], taps, 0, back)
        return carry

    lax.fori_loop(0, rows // STEP, chunk, 0)


def hidden_kernel(lengths, z, query, recv, head, taps, bands, gain, out, ext, first_q):
    me = stretch_id()
    rows, width = z.shape
    back = reach_back(lengths, me * rows, (TAIL, width))
    fixed = []
    for i in range(3):
        tail = recv[HALF + i * TAIL : HALF + (i + 1) * TAIL, :].astype(F32)
        mine = head[i * TAIL : (i + 1) * TAIL, :].astype(F32)
        fixed.append(short_rows(jnp.concatenate([tail, mine], axis=0), taps, i, back))
    first = (fixed[1] * fixed[2]).astype(BF16).astype(F32)
    ext[0:HALF, :] = recv[0:HALF, :]
    ext[HALF:, :] = z[...]
    later = z[TAIL : 2 * TAIL, :].astype(F32)
    ext[HALF : HALF + 2 * TAIL, :] = jnp.concatenate([first, later], axis=0).astype(BF16)
    first_q[0:TAIL, :] = fixed[0]
    first_q[TAIL:, :] = query[TAIL:HALF, :]
    lane = 128
    per = lane // (width // bands.shape[0])
    group = lax.broadcasted_iota(jnp.int32, (HALF, lane), 1) // (lane // per)
    for b in range(rows // HALF):
        back = reach_back(lengths, me * rows + b * HALF, (HALF, 2 * HALF))
        i = lax.broadcasted_iota(jnp.int32, (HALF, 2 * HALF), 0)
        p = lax.broadcasted_iota(jnp.int32, (HALF, 2 * HALF), 1)
        keep = jnp.where(i + HALF - p <= back, 1.0, 0.0).astype(BF16)
        for t in range(width // lane):
            cols = slice(t * lane, (t + 1) * lane)
            right = ext[b * HALF : (b + 2) * HALF, cols]
            total = jnp.zeros((HALF, lane), F32)
            for g in range(per):
                got = jnp.dot(bands[t * per + g] * keep, right, preferred_element_type=F32)
                total = jnp.where(group == g, got, total)
            zs = ext[(b + 1) * HALF : (b + 2) * HALF, cols].astype(F32)
            q = first_q[:, cols] if b == 0 else query[b * HALF : (b + 1) * HALF, cols]
            value = (q * (total + gain[:, cols] * zs)).astype(BF16)
            for copy in range(out.shape[0]):
                out[copy, b * HALF : (b + 1) * HALF, cols] = value


def relay_kernel(up, down, up_out, down_out):
    up_out[...] = up[...]
    down_out[...] = down[...]


def project_kernel(offsets, part, own, other, *refs):
    weights, (same, cross) = refs[:-2], refs[-2:]
    count, rows, lane = same.shape[1:]
    n = len(weights) - 1
    y = lax.axis_index("y")
    at = slice(part * count * rows, (part + 1) * count * rows)
    left = jnp.concatenate([own[at, :], other[at, :]], axis=1)
    blocks = [w[...] for w in weights[:-2]]
    blocks.append(jnp.concatenate([weights[-2][...], weights[-1][...]], axis=0))
    for pair in range(0, n, 2):
        wide = jnp.concatenate(blocks[pair : pair + 2], axis=1)
        got = jnp.dot(left, wide, preferred_element_type=F32).astype(BF16)
        for i in range(2):
            owner = lax.rem(y - offsets[pair + i] + n, n)
            high = lax.div(owner, 2)
            odd = lax.rem(owner + lax.axis_index("zl"), 2)
            piece = got[:, i * lane : (i + 1) * lane].reshape(count, rows, lane)

            @pl.when(odd == 0)
            def _():
                same[high] = piece

            @pl.when(odd == 1)
            def _():
                cross[high] = piece


def project(part, own, other, weights, nx):
    rows = own.shape[0] // nx
    blocks = [w[1] for w in weights]
    lane = blocks[0].shape[1]
    return call(
        functools.partial(project_kernel, tuple(w[0] for w in weights), part),
        [shape(((len(blocks) - 1) // 2, nx // 2, rows, lane))] * 2,
        [vmem()] * (2 + len(blocks)),
        (own, other, *blocks),
        2 * own.size * 8 * lane,
    )


def pair_kernel(own0, own1, got0, got1, out):
    count = own0.shape[1]

    def one(z, carry):
        for i, (own, got) in enumerate(((own0, got0), (own1, got1))):
            for s in range(count):
                total = own[z, s].astype(F32) + got[z, s].astype(F32)
                out[z, i * count + s] = total.astype(BF16)
        return carry

    lax.fori_loop(0, own0.shape[0], one, 0)


def along_z(block, distance):
    n = lax.axis_size(("zh", "zl"))
    return lax.ppermute(block, ("zh", "zl"), [(i, (i + distance) % n) for i in range(n)])


def summed(parts):
    columns = [jnp.sum(parts[:, x].astype(F32), axis=0) for x in range(parts.shape[1])]
    return jnp.concatenate(columns, axis=1).astype(BF16)


def shape(dims, dtype=BF16):
    return jax.ShapeDtypeStruct(dims, dtype)


def passed_along(block):
    n = lax.axis_size(CTX)
    return lax.ppermute(block, CTX, [(i, i + 1) for i in range(n - 1)])


def weight_columns(out_weight):
    nx = lax.axis_size("x")
    core = lax.axis_index("core")
    width = out_weight.shape[1] // 2
    halves = (out_weight[:, :width], out_weight[:, width:])
    same = jnp.where(core == 0, halves[0], halves[1])
    flip = jnp.where(core == 0, halves[1], halves[0])
    route = lambda f: [
        (x * 2 + i, (2 * (x % 2) + f(i)) * 2 + x // 2) for x in range(nx) for i in range(2)
    ]
    a = lax.ppermute(same, ("x", "core"), route(lambda i: i))
    b = lax.ppermute(flip, ("x", "core"), route(lambda i: 1 - i))
    straight = lax.axis_index("x") % 2 == core
    own = jnp.where(straight, a, b)
    other = jnp.where(straight, b, a)
    return jnp.concatenate([own, other], axis=0)


def around(block, distance):
    n = lax.axis_size("y")
    return lax.ppermute(block, "y", [(i, (i + distance) % n) for i in range(n)])


def operator(
    source_rows,
    short_filters,
    medium_filters,
    skip_gain,
    out_weight,
    doc_lengths,
    block_packing_device,
):
    ny, nx = lax.axis_size("y"), lax.axis_size("x")
    stretches = ny * nx
    width = source_rows.shape[2]
    rows = block_packing_device.shape[1] * BLK
    bpd = block_packing_device.T

    packed = packed_blocks(bpd, source_rows.transpose(1, 0, 2), stretches)
    blocks = lax.all_to_all(packed, CTX, split_axis=0, concat_axis=0, tiled=True)

    block = weight_columns(out_weight)
    up, down = around(block, 1), around(block, -1)
    up2, down2 = around(up, 1), around(down, -1)
    weights = [(0, block), (1, up), (-1, down), (2, up2), (-2, down2)]
    both = [shape(up.shape)] * 2
    up, down = call(relay_kernel, both, [vmem()] * 2, (up, down), 0)
    cut = up.shape[0] // 2
    weights += [(3, around(up, 2)), (-3, around(down, -2))]
    weights += [(4, around(up[:cut], 3)), (4, around(down[cut:], -3))]

    groups = medium_filters.shape[1]
    line = jnp.pad(medium_filters[::-1].T.astype(F32), ((0, 0), (1, HALF - 1)))
    (bands,) = call(toeplitz_kernel, [shape((groups, HALF, 2 * HALF))], [vmem()], (line,), 10**8)

    z, send, head = call(
        gated_kernel,
        [shape((rows, width)), shape((HALF + 3 * TAIL, width)), shape((3 * TAIL, width))],
        [smem(), smem(), vmem(), vmem()],
        (bpd, doc_lengths, blocks, short_filters),
        10**7,
        scratch=[pltpu.VMEM((2, rows + TAIL, width), F32)],
    )
    recv = passed_along(send)
    (query,) = call(
        query_kernel,
        [shape((rows, width), F32)],
        [smem(), smem(), vmem(), vmem()],
        (bpd, doc_lengths, blocks, short_filters),
        10**7,
        scratch=[pltpu.VMEM((rows + TAIL, width), F32)],
    )
    gain = skip_gain.reshape(1, width)
    (copies,) = call(
        hidden_kernel,
        [shape((nx, rows, width))],
        [smem()] + [vmem()] * 7,
        (doc_lengths, z, query, recv, head, short_filters, bands, gain),
        10**9,
        scratch=[pltpu.VMEM((rows + HALF, width), BF16), pltpu.VMEM((HALF, width), F32)],
    )
    own = lax.all_to_all(copies, "x", split_axis=0, concat_axis=0, tiled=True)
    own = own.reshape(nx * rows, width)
    other = lax.ppermute(own, "core", [(0, 1), (1, 0)])
    mine, got = [], []
    for part, distance in ((0, 1), (1, -1)):
        same, cross = project(part, own, other, weights, nx)
        mine.append(same)
        got.append(along_z(cross, distance))
    nzh, _, _, lane = mine[0].shape
    (pairs,) = call(pair_kernel, [shape((nzh, nx, rows, lane))], [vmem()] * 4, (*mine, *got), 10**6)
    flat = pairs.reshape(nzh * nx, rows, lane)
    parts = lax.all_to_all(flat, ("zh", "x"), split_axis=0, concat_axis=0, tiled=True)
    return summed(parts.reshape(pairs.shape))


def solution(mesh):
    ctx, mp = CTX, ("zh", "zl", "core")
    mesh5 = Mesh(mesh.devices.reshape(SHAPE5), ctx + mp)
    return jax.shard_map(
        operator,
        mesh=mesh5,
        in_specs=(
            P(ctx, None, mp),
            P(None, None, mp),
            P(None, mp),
            P(mp),
            P(mp, ctx),
            P(),
            P(),
        ),
        out_specs=P(ctx, mp),
        check_vma=False,
    )
```

```python
import functools

import jax
import jax.numpy as jnp
from jax import lax
from jax.experimental import pallas as pl
from jax.experimental.pallas import tpu as pltpu
from jax.sharding import Mesh, PartitionSpec as P


CTX = ("y", "x")
SHAPE5 = (8, 4, 4, 2, 2)
BLK = 16
TAIL = 8
GRANT = 24 << 20
HALF = 128
F32, BF16 = jnp.float32, jnp.bfloat16


def smem():
    return pl.BlockSpec(memory_space=pltpu.SMEM)


def vmem():
    return pl.BlockSpec(memory_space=pltpu.VMEM)


def stretch_id():
    return lax.axis_index("y") * lax.axis_size("x") + lax.axis_index("x")


def call(body, outs, ins, args, flops, scratch=()):
    moved = sum(a.size * a.dtype.itemsize for a in args)
    moved += sum(o.size * o.dtype.itemsize for o in outs)
    return pl.pallas_call(
        body,
        out_shape=outs,
        in_specs=ins,
        out_specs=[vmem()] * len(outs),
        scratch_shapes=list(scratch),
        compiler_params=pltpu.CompilerParams(vmem_limit_bytes=GRANT),
        cost_estimate=pl.CostEstimate(flops=flops, bytes_accessed=moved, transcendentals=0),
    )(*args)


def reach_back(lengths, first, shape):
    at = first + lax.broadcasted_iota(jnp.int32, shape, 0)
    begin = jnp.zeros(shape, jnp.int32)
    start = jnp.int32(0)
    for doc in range(lengths.shape[0]):
        begin = jnp.where(at >= start, start, begin)
        start = start + lengths[doc]
    return at - begin


def short_rows(window, taps_ref, which, back):
    count = back.shape[0]
    total = jnp.zeros(back.shape, F32)
    for step in range(taps_ref.shape[1]):
        tap = taps_ref[which, step : step + 1, :].astype(F32)
        piece = window[TAIL - step : TAIL - step + count]
        total = total + jnp.where(back >= step, tap * piece, 0.0)
    return total


def pack_kernel(bpd, src, out, sem):
    me = stretch_id()

    def one(c, slot):
        mine = bpd[0, c] == me
        for k in range(1, bpd.shape[0]):
            mine = mine | (bpd[k, c] == me)
        rows = pl.ds(pl.multiple_of(slot * BLK, BLK), BLK)
        pltpu.make_async_copy(src.at[:, rows, :], out.at[c], sem).start()
        return slot + mine.astype(jnp.int32)

    lax.fori_loop(0, bpd.shape[1], one, jnp.int32(0), unroll=2)
    pltpu.make_async_copy(out, out, sem).wait()


def packed_blocks(bpd, src, stretches):
    return pl.pallas_call(
        pack_kernel,
        in_specs=[smem(), vmem()],
        out_specs=pl.BlockSpec(memory_space=pl.ANY),
        out_shape=shape((stretches, 3, BLK, src.shape[2])),
        scratch_shapes=[pltpu.SemaphoreType.DMA],
        cost_estimate=pl.CostEstimate(
            flops=10**6, bytes_accessed=4 * src.size, transcendentals=0
        ),
        name="pack",
    )(bpd, src)


def toeplitz_kernel(line, out):
    def one(g, carry):
        row = jnp.broadcast_to(line[pl.ds(g, 1), :], out.shape[1:])
        out[g] = pltpu.roll(row, 0, 1, stride=1, stride_axis=0).astype(BF16)
        return carry

    lax.fori_loop(0, out.shape[0], one, 0, unroll=4)


def gather_rows(bpd, blocks, which, buf):
    me = stretch_id()
    buf[0:TAIL, :] = jnp.zeros((TAIL, buf.shape[1]), F32)
    for k in range((buf.shape[0] - TAIL) // BLK):
        buf[TAIL + k * BLK : TAIL + (k + 1) * BLK, :] = blocks[bpd[k, me], which].astype(F32)


STEP = 32


def gated_kernel(bpd, lengths, blocks, taps, z, send, head, buf):
    me = stretch_id()
    rows, width = z.shape
    for i in range(2):
        gather_rows(bpd, blocks, 1 + i, buf.at[i])

    def chunk(r, carry):
        at = pl.multiple_of(r * STEP, STEP)
        back = reach_back(lengths, me * rows + at, (STEP, width))
        wide = pl.ds(at, STEP + TAIL)
        keyed = short_rows(buf[0, wide, :], taps, 1, back)
        valued = short_rows(buf[1, wide, :], taps, 2, back)
        z[pl.ds(at, STEP), :] = (keyed * valued).astype(BF16)
        return carry

    lax.fori_loop(0, rows // STEP, chunk, 0)
    send[0:HALF, :] = z[rows - HALF :, :]
    q_last = blocks[bpd[rows // BLK - 1, me], 0].astype(F32)[BLK - TAIL :]
    q_first = blocks[bpd[0, me], 0].astype(F32)[:TAIL]
    tails = [q_last] + [buf[i, rows : rows + TAIL, :] for i in range(2)]
    heads = [q_first] + [buf[i, TAIL : 2 * TAIL, :] for i in range(2)]
    for i in range(3):
        send[HALF + i * TAIL : HALF + (i + 1) * TAIL, :] = tails[i].astype(BF16)
        head[i * TAIL : (i + 1) * TAIL, :] = heads[i].astype(BF16)


def query_kernel(bpd, lengths, blocks, taps, out, buf):
    me = stretch_id()
    rows, width = out.shape
    gather_rows(bpd, blocks, 0, buf)

    def chunk(r, carry):
        at = pl.multiple_of(r * STEP, STEP)
        back = reach_back(lengths, me * rows + at, (STEP, width))
        out[pl.ds(at, STEP), :] = short_rows(buf[pl.ds(at, STEP + TAIL), :], taps, 0, back)
        return carry

    lax.fori_loop(0, rows // STEP, chunk, 0)


def hidden_kernel(lengths, z, query, recv, head, taps, bands, gain, out, ext, first_q):
    me = stretch_id()
    rows, width = z.shape
    back = reach_back(lengths, me * rows, (TAIL, width))
    fixed = []
    for i in range(3):
        tail = recv[HALF + i * TAIL : HALF + (i + 1) * TAIL, :].astype(F32)
        mine = head[i * TAIL : (i + 1) * TAIL, :].astype(F32)
        fixed.append(short_rows(jnp.concatenate([tail, mine], axis=0), taps, i, back))
    first = (fixed[1] * fixed[2]).astype(BF16).astype(F32)
    ext[0:HALF, :] = recv[0:HALF, :]
    ext[HALF:, :] = z[...]
    later = z[TAIL : 2 * TAIL, :].astype(F32)
    ext[HALF : HALF + 2 * TAIL, :] = jnp.concatenate([first, later], axis=0).astype(BF16)
    first_q[0:TAIL, :] = fixed[0]
    first_q[TAIL:, :] = query[TAIL:HALF, :]
    lane = 128
    per = lane // (width // bands.shape[0])
    group = lax.broadcasted_iota(jnp.int32, (HALF, lane), 1) // (lane // per)
    for b in range(rows // HALF):
        back = reach_back(lengths, me * rows + b * HALF, (HALF, 2 * HALF))
        i = lax.broadcasted_iota(jnp.int32, (HALF, 2 * HALF), 0)
        p = lax.broadcasted_iota(jnp.int32, (HALF, 2 * HALF), 1)
        keep = jnp.where(i + HALF - p <= back, 1.0, 0.0).astype(BF16)
        for t in range(width // lane):
            cols = slice(t * lane, (t + 1) * lane)
            right = ext[b * HALF : (b + 2) * HALF, cols]
            total = jnp.zeros((HALF, lane), F32)
            for g in range(per):
                got = jnp.dot(bands[t * per + g] * keep, right, preferred_element_type=F32)
                total = jnp.where(group == g, got, total)
            zs = ext[(b + 1) * HALF : (b + 2) * HALF, cols].astype(F32)
            q = first_q[:, cols] if b == 0 else query[b * HALF : (b + 1) * HALF, cols]
            value = (q * (total + gain[:, cols] * zs)).astype(BF16)
            for copy in range(out.shape[0]):
                out[copy, b * HALF : (b + 1) * HALF, cols] = value


def join_kernel(block, up, down, up_out, down_out):
    rows = block.shape[0]
    for first, out in ((up, up_out), (down, down_out)):
        out[:rows] = block[...]
        out[rows:] = first[...]


def halve_kernel(up, down, up_out, down_out):
    rows = up_out.shape[0]
    up_out[...] = up[:rows]
    down_out[...] = down[rows:]


DISTANCES = ((0, 2, -2, 4), (1, -1, 3, -3))


def project_kernel(parts, cross, own, other, *refs):
    block, up, down, up23, down23, up4, down4 = refs[:7]
    outs = refs[7:]
    count, rows, lane = outs[0].shape[1:]
    k = block.shape[0]
    n = 2 * outs[0].shape[0]
    load = {
        0: lambda: block[...],
        1: lambda: up[...],
        -1: lambda: down[...],
        2: lambda: up23[:k],
        3: lambda: up23[k:],
        -2: lambda: down23[:k],
        -3: lambda: down23[k:],
        4: lambda: jnp.concatenate([up4[...], down4[...]], axis=0),
    }
    y = lax.axis_index("y")
    parity = lax.rem(y + lax.axis_index("zl"), 2)

    def fill(distances):
        for part, out in zip(parts, outs):
            at = slice(part * count * rows, (part + 1) * count * rows)
            left = jnp.concatenate([own[at, :], other[at, :]], axis=1)
            for pair in (distances[:2], distances[2:]):
                wide = jnp.concatenate([load[d]() for d in pair], axis=1)
                got = jnp.dot(left, wide, preferred_element_type=F32).astype(BF16)
                for i, d in enumerate(pair):
                    high = lax.div(lax.rem(y - d + n, n), 2)
                    piece = got[:, i * lane : (i + 1) * lane]
                    out[high] = piece.reshape(count, rows, lane)

    for odd in range(2):

        @pl.when(lax.rem(parity + odd, 2) == cross)
        def _():
            fill(DISTANCES[odd])


def project(parts, cross, own, other, weights, nx):
    rows = own.shape[0] // nx
    lane = weights[0].shape[1]
    return call(
        functools.partial(project_kernel, parts, cross),
        [shape((len(DISTANCES[0]), nx // 2, rows, lane))] * len(parts),
        [vmem()] * (2 + len(weights)),
        (own, other, *weights),
        4 * own.size * 2 * len(parts) * lane,
    )


def pair_kernel(own0, own1, got0, got1, out):
    count = own0.shape[1]

    def one(z, carry):
        for i, (own, got) in enumerate(((own0, got0), (own1, got1))):
            for s in range(count):
                total = own[z, s].astype(F32) + got[z, s].astype(F32)
                out[z, i * count + s] = total.astype(BF16)
        return carry

    lax.fori_loop(0, own0.shape[0], one, 0)


def along_z(block, distance):
    n = lax.axis_size(("zh", "zl"))
    return lax.ppermute(block, ("zh", "zl"), [(i, (i + distance) % n) for i in range(n)])


def summed(parts):
    columns = [jnp.sum(parts[:, x].astype(F32), axis=0) for x in range(parts.shape[1])]
    return jnp.concatenate(columns, axis=1).astype(BF16)


def shape(dims, dtype=BF16):
    return jax.ShapeDtypeStruct(dims, dtype)


def passed_along(block):
    n = lax.axis_size(CTX)
    return lax.ppermute(block, CTX, [(i, i + 1) for i in range(n - 1)])


def weight_columns(out_weight):
    nx = lax.axis_size("x")
    core = lax.axis_index("core")
    width = out_weight.shape[1] // 2
    halves = (out_weight[:, :width], out_weight[:, width:])
    same = jnp.where(core == 0, halves[0], halves[1])
    flip = jnp.where(core == 0, halves[1], halves[0])
    route = lambda f: [
        (x * 2 + i, (2 * (x % 2) + f(i)) * 2 + x // 2) for x in range(nx) for i in range(2)
    ]
    a = lax.ppermute(same, ("x", "core"), route(lambda i: i))
    b = lax.ppermute(flip, ("x", "core"), route(lambda i: 1 - i))
    straight = lax.axis_index("x") % 2 == core
    own = jnp.where(straight, a, b)
    other = jnp.where(straight, b, a)
    return jnp.concatenate([own, other], axis=0)


def around(block, distance):
    n = lax.axis_size("y")
    return lax.ppermute(block, "y", [(i, (i + distance) % n) for i in range(n)])


def operator(
    source_rows,
    short_filters,
    medium_filters,
    skip_gain,
    out_weight,
    doc_lengths,
    block_packing_device,
):
    ny, nx = lax.axis_size("y"), lax.axis_size("x")
    stretches = ny * nx
    width = source_rows.shape[2]
    rows = block_packing_device.shape[1] * BLK
    bpd = block_packing_device.T

    packed = packed_blocks(bpd, source_rows.transpose(1, 0, 2), stretches)
    blocks = lax.all_to_all(packed, CTX, split_axis=0, concat_axis=0, tiled=True)

    block = weight_columns(out_weight)
    up, down = around(block, 1), around(block, -1)
    double = [shape((2 * block.shape[0], block.shape[1]))] * 2
    ups, downs = call(join_kernel, double, [vmem()] * 3, (block, up, down), 0)
    up23, down23 = around(ups, 2), around(downs, -2)
    half = [shape((block.shape[0] // 2, block.shape[1]))] * 2
    up4, down4 = call(halve_kernel, half, [vmem()] * 2, (up, down), 0)
    up4, down4 = around(up4, 3), around(down4, -3)
    weights = (block, up, down, up23, down23, up4, down4)

    groups = medium_filters.shape[1]
    line = jnp.pad(medium_filters[::-1].T.astype(F32), ((0, 0), (1, HALF - 1)))
    (bands,) = call(toeplitz_kernel, [shape((groups, HALF, 2 * HALF))], [vmem()], (line,), 10**8)

    z, send, head = call(
        gated_kernel,
        [shape((rows, width)), shape((HALF + 3 * TAIL, width)), shape((3 * TAIL, width))],
        [smem(), smem(), vmem(), vmem()],
        (bpd, doc_lengths, blocks, short_filters),
        10**7,
        scratch=[pltpu.VMEM((2, rows + TAIL, width), F32)],
    )
    recv = passed_along(send)
    (query,) = call(
        query_kernel,
        [shape((rows, width), F32)],
        [smem(), smem(), vmem(), vmem()],
        (bpd, doc_lengths, blocks, short_filters),
        10**7,
        scratch=[pltpu.VMEM((rows + TAIL, width), F32)],
    )
    gain = skip_gain.reshape(1, width)
    (copies,) = call(
        hidden_kernel,
        [shape((nx, rows, width))],
        [smem()] + [vmem()] * 7,
        (doc_lengths, z, query, recv, head, short_filters, bands, gain),
        10**9,
        scratch=[pltpu.VMEM((rows + HALF, width), BF16), pltpu.VMEM((HALF, width), F32)],
    )
    own = lax.all_to_all(copies, "x", split_axis=0, concat_axis=0, tiled=True)
    own = own.reshape(nx * rows, width)
    other = lax.ppermute(own, "core", [(0, 1), (1, 0)])
    got = []
    for part, distance in ((0, 1), (1, -1)):
        (cross,) = project((part,), 1, own, other, weights, nx)
        got.append(along_z(cross, distance))
    mine = project((0, 1), 0, own, other, weights, nx)
    nzh, half, _, lane = mine[0].shape
    (pairs,) = call(pair_kernel, [shape((nzh, nx, rows, lane))], [vmem()] * 4, (*mine, *got), 10**6)
    flat = pairs.reshape(nzh * nx, rows, lane)
    parts = lax.all_to_all(flat, ("zh", "x"), split_axis=0, concat_axis=0, tiled=True)
    return summed(parts.reshape(pairs.shape))


def solution(mesh):
    ctx, mp = CTX, ("zh", "zl", "core")
    mesh5 = Mesh(mesh.devices.reshape(SHAPE5), ctx + mp)
    return jax.shard_map(
        operator,
        mesh=mesh5,
        in_specs=(
            P(ctx, None, mp),
            P(None, None, mp),
            P(None, mp),
            P(mp),
            P(mp, ctx),
            P(),
            P(),
        ),
        out_specs=P(ctx, mp),
        check_vma=False,
    )
```

```python
import functools

import jax
import jax.numpy as jnp
from jax import lax
from jax.experimental import pallas as pl
from jax.experimental.pallas import tpu as pltpu
from jax.sharding import Mesh, PartitionSpec as P


CTX = ("y", "x")
SHAPE5 = (8, 4, 4, 2, 2)
BLK = 16
TAIL = 8
GRANT = 24 << 20
HALF = 128
F32, BF16 = jnp.float32, jnp.bfloat16


def smem():
    return pl.BlockSpec(memory_space=pltpu.SMEM)


def vmem():
    return pl.BlockSpec(memory_space=pltpu.VMEM)


def stretch_id():
    return lax.axis_index("y") * lax.axis_size("x") + lax.axis_index("x")


def call(body, outs, ins, args, flops, scratch=()):
    moved = sum(a.size * a.dtype.itemsize for a in args)
    moved += sum(o.size * o.dtype.itemsize for o in outs)
    return pl.pallas_call(
        body,
        out_shape=outs,
        in_specs=ins,
        out_specs=[vmem()] * len(outs),
        scratch_shapes=list(scratch),
        compiler_params=pltpu.CompilerParams(vmem_limit_bytes=GRANT),
        cost_estimate=pl.CostEstimate(flops=flops, bytes_accessed=moved, transcendentals=0),
    )(*args)


def reach_back(lengths, first, shape):
    at = first + lax.broadcasted_iota(jnp.int32, shape, 0)
    begin = jnp.zeros(shape, jnp.int32)
    start = jnp.int32(0)
    for doc in range(lengths.shape[0]):
        begin = jnp.where(at >= start, start, begin)
        start = start + lengths[doc]
    return at - begin


def short_rows(window, taps_ref, which, back):
    count = back.shape[0]
    total = jnp.zeros(back.shape, F32)
    for step in range(taps_ref.shape[1]):
        tap = taps_ref[which, step : step + 1, :].astype(F32)
        piece = window[TAIL - step : TAIL - step + count]
        total = total + jnp.where(back >= step, tap * piece, 0.0)
    return total


def pack_kernel(bpd, src, out, sem):
    me = stretch_id()

    def one(c, slot):
        mine = bpd[0, c] == me
        for k in range(1, bpd.shape[0]):
            mine = mine | (bpd[k, c] == me)
        rows = pl.ds(pl.multiple_of(slot * BLK, BLK), BLK)
        pltpu.make_async_copy(src.at[:, rows, :], out.at[c], sem).start()
        return slot + mine.astype(jnp.int32)

    lax.fori_loop(0, bpd.shape[1], one, jnp.int32(0), unroll=2)
    pltpu.make_async_copy(out, out, sem).wait()


def packed_blocks(bpd, src, stretches):
    return pl.pallas_call(
        pack_kernel,
        in_specs=[smem(), vmem()],
        out_specs=pl.BlockSpec(memory_space=pl.ANY),
        out_shape=shape((stretches, 3, BLK, src.shape[2])),
        scratch_shapes=[pltpu.SemaphoreType.DMA],
        cost_estimate=pl.CostEstimate(
            flops=10**6, bytes_accessed=4 * src.size, transcendentals=0
        ),
        name="pack",
    )(bpd, src)


def toeplitz_kernel(line, out):
    def one(g, carry):
        row = jnp.broadcast_to(line[pl.ds(g, 1), :], out.shape[1:])
        out[g] = pltpu.roll(row, 0, 1, stride=1, stride_axis=0).astype(BF16)
        return carry

    lax.fori_loop(0, out.shape[0], one, 0, unroll=4)


def gather_rows(bpd, blocks, which, buf):
    me = stretch_id()
    buf[0:TAIL, :] = jnp.zeros((TAIL, buf.shape[1]), F32)
    for k in range((buf.shape[0] - TAIL) // BLK):
        buf[TAIL + k * BLK : TAIL + (k + 1) * BLK, :] = blocks[bpd[k, me], which].astype(F32)


STEP = 32


def gated_kernel(bpd, lengths, blocks, taps, z, send, head, buf):
    me = stretch_id()
    rows, width = z.shape
    for i in range(2):
        gather_rows(bpd, blocks, 1 + i, buf.at[i])

    def chunk(r, carry):
        at = pl.multiple_of(r * STEP, STEP)
        back = reach_back(lengths, me * rows + at, (STEP, width))
        wide = pl.ds(at, STEP + TAIL)
        keyed = short_rows(buf[0, wide, :], taps, 1, back)
        valued = short_rows(buf[1, wide, :], taps, 2, back)
        z[pl.ds(at, STEP), :] = (keyed * valued).astype(BF16)
        return carry

    lax.fori_loop(0, rows // STEP, chunk, 0)
    send[0:HALF, :] = z[rows - HALF :, :]
    q_last = blocks[bpd[rows // BLK - 1, me], 0].astype(F32)[BLK - TAIL :]
    q_first = blocks[bpd[0, me], 0].astype(F32)[:TAIL]
    tails = [q_last] + [buf[i, rows : rows + TAIL, :] for i in range(2)]
    heads = [q_first] + [buf[i, TAIL : 2 * TAIL, :] for i in range(2)]
    for i in range(3):
        send[HALF + i * TAIL : HALF + (i + 1) * TAIL, :] = tails[i].astype(BF16)
        head[i * TAIL : (i + 1) * TAIL, :] = heads[i].astype(BF16)


def query_kernel(bpd, lengths, blocks, taps, out, buf):
    me = stretch_id()
    rows, width = out.shape
    gather_rows(bpd, blocks, 0, buf)

    def chunk(r, carry):
        at = pl.multiple_of(r * STEP, STEP)
        back = reach_back(lengths, me * rows + at, (STEP, width))
        out[pl.ds(at, STEP), :] = short_rows(buf[pl.ds(at, STEP + TAIL), :], taps, 0, back)
        return carry

    lax.fori_loop(0, rows // STEP, chunk, 0)


def hidden_kernel(lengths, z, query, recv, head, taps, bands, gain, out, ext, first_q):
    me = stretch_id()
    rows, width = z.shape
    back = reach_back(lengths, me * rows, (TAIL, width))
    fixed = []
    for i in range(3):
        tail = recv[HALF + i * TAIL : HALF + (i + 1) * TAIL, :].astype(F32)
        mine = head[i * TAIL : (i + 1) * TAIL, :].astype(F32)
        fixed.append(short_rows(jnp.concatenate([tail, mine], axis=0), taps, i, back))
    first = (fixed[1] * fixed[2]).astype(BF16).astype(F32)
    ext[0:HALF, :] = recv[0:HALF, :]
    ext[HALF:, :] = z[...]
    later = z[TAIL : 2 * TAIL, :].astype(F32)
    ext[HALF : HALF + 2 * TAIL, :] = jnp.concatenate([first, later], axis=0).astype(BF16)
    first_q[0:TAIL, :] = fixed[0]
    first_q[TAIL:, :] = query[TAIL:HALF, :]
    lane = 128
    per = lane // (width // bands.shape[0])
    group = lax.broadcasted_iota(jnp.int32, (HALF, lane), 1) // (lane // per)
    for b in range(rows // HALF):
        back = reach_back(lengths, me * rows + b * HALF, (HALF, 2 * HALF))
        i = lax.broadcasted_iota(jnp.int32, (HALF, 2 * HALF), 0)
        p = lax.broadcasted_iota(jnp.int32, (HALF, 2 * HALF), 1)
        keep = jnp.where(i + HALF - p <= back, 1.0, 0.0).astype(BF16)
        for t in range(width // lane):
            cols = slice(t * lane, (t + 1) * lane)
            right = ext[b * HALF : (b + 2) * HALF, cols]
            total = jnp.zeros((HALF, lane), F32)
            for g in range(per):
                got = jnp.dot(bands[t * per + g] * keep, right, preferred_element_type=F32)
                total = jnp.where(group == g, got, total)
            zs = ext[(b + 1) * HALF : (b + 2) * HALF, cols].astype(F32)
            q = first_q[:, cols] if b == 0 else query[b * HALF : (b + 1) * HALF, cols]
            value = (q * (total + gain[:, cols] * zs)).astype(BF16)
            for copy in range(out.shape[0]):
                out[copy, b * HALF : (b + 1) * HALF, cols] = value


def relay_kernel(up, down, up_out, down_out, up_half, down_half):
    rows = up_half.shape[0]
    up_out[...] = up[...]
    down_out[...] = down[...]
    up_half[...] = up[:rows]
    down_half[...] = down[rows:]


DISTANCES = ((0, 2, -2, 4), (1, -1, 3, -3))


def project_kernel(parts, cross, own, other, *refs):
    block, up, down, up2, down2, up3, down3, up4, down4 = refs[:9]
    outs = refs[9:]
    count, rows, lane = outs[0].shape[1:]
    n = 2 * outs[0].shape[0]
    load = {
        0: lambda: block[...],
        1: lambda: up[...],
        -1: lambda: down[...],
        2: lambda: up2[...],
        -2: lambda: down2[...],
        3: lambda: up3[...],
        -3: lambda: down3[...],
        4: lambda: jnp.concatenate([up4[...], down4[...]], axis=0),
    }
    y = lax.axis_index("y")
    parity = lax.rem(y + lax.axis_index("zl"), 2)

    def fill(distances):
        for part, out in zip(parts, outs):
            at = slice(part * count * rows, (part + 1) * count * rows)
            left = jnp.concatenate([own[at, :], other[at, :]], axis=1)
            for pair in (distances[:2], distances[2:]):
                wide = jnp.concatenate([load[d]() for d in pair], axis=1)
                got = jnp.dot(left, wide, preferred_element_type=F32).astype(BF16)
                for i, d in enumerate(pair):
                    high = lax.div(lax.rem(y - d + n, n), 2)
                    piece = got[:, i * lane : (i + 1) * lane]
                    out[high] = piece.reshape(count, rows, lane)

    for odd in range(2):

        @pl.when(lax.rem(parity + odd, 2) == cross)
        def _():
            fill(DISTANCES[odd])


def project(parts, cross, own, other, weights, nx):
    rows = own.shape[0] // nx
    lane = weights[0].shape[1]
    return call(
        functools.partial(project_kernel, parts, cross),
        [shape((len(DISTANCES[0]), nx // 2, rows, lane))] * len(parts),
        [vmem()] * (2 + len(weights)),
        (own, other, *weights),
        4 * own.size * 2 * len(parts) * lane,
    )


def pair_kernel(own0, own1, got0, got1, out):
    count = own0.shape[1]

    def one(z, carry):
        for i, (own, got) in enumerate(((own0, got0), (own1, got1))):
            for s in range(count):
                total = own[z, s].astype(F32) + got[z, s].astype(F32)
                out[z, i * count + s] = total.astype(BF16)
        return carry

    lax.fori_loop(0, own0.shape[0], one, 0)


def along_z(block, distance):
    n = lax.axis_size(("zh", "zl"))
    return lax.ppermute(block, ("zh", "zl"), [(i, (i + distance) % n) for i in range(n)])


def summed(parts):
    columns = [jnp.sum(parts[:, x].astype(F32), axis=0) for x in range(parts.shape[1])]
    return jnp.concatenate(columns, axis=1).astype(BF16)


def shape(dims, dtype=BF16):
    return jax.ShapeDtypeStruct(dims, dtype)


def passed_along(block):
    n = lax.axis_size(CTX)
    return lax.ppermute(block, CTX, [(i, i + 1) for i in range(n - 1)])


def weight_columns(out_weight):
    nx = lax.axis_size("x")
    core = lax.axis_index("core")
    width = out_weight.shape[1] // 2
    halves = (out_weight[:, :width], out_weight[:, width:])
    same = jnp.where(core == 0, halves[0], halves[1])
    flip = jnp.where(core == 0, halves[1], halves[0])
    route = lambda f: [
        (x * 2 + i, (2 * (x % 2) + f(i)) * 2 + x // 2) for x in range(nx) for i in range(2)
    ]
    a = lax.ppermute(same, ("x", "core"), route(lambda i: i))
    b = lax.ppermute(flip, ("x", "core"), route(lambda i: 1 - i))
    straight = lax.axis_index("x") % 2 == core
    own = jnp.where(straight, a, b)
    other = jnp.where(straight, b, a)
    return jnp.concatenate([own, other], axis=0)


def around(block, distance):
    n = lax.axis_size("y")
    return lax.ppermute(block, "y", [(i, (i + distance) % n) for i in range(n)])


def operator(
    source_rows,
    short_filters,
    medium_filters,
    skip_gain,
    out_weight,
    doc_lengths,
    block_packing_device,
):
    ny, nx = lax.axis_size("y"), lax.axis_size("x")
    stretches = ny * nx
    width = source_rows.shape[2]
    rows = block_packing_device.shape[1] * BLK
    bpd = block_packing_device.T

    packed = packed_blocks(bpd, source_rows.transpose(1, 0, 2), stretches)
    blocks = lax.all_to_all(packed, CTX, split_axis=0, concat_axis=0, tiled=True)

    block = weight_columns(out_weight)
    up, down = around(block, 1), around(block, -1)
    up2, down2 = around(block, 2), around(block, -2)
    whole = shape(block.shape)
    half = shape((block.shape[0] // 2, block.shape[1]))
    relayed = call(relay_kernel, [whole, whole, half, half], [vmem()] * 2, (up2, down2), 0)
    up3, down3 = around(relayed[0], 1), around(relayed[1], -1)
    up4, down4 = around(relayed[2], 2), around(relayed[3], -2)
    weights = (block, up, down, up2, down2, up3, down3, up4, down4)

    groups = medium_filters.shape[1]
    line = jnp.pad(medium_filters[::-1].T.astype(F32), ((0, 0), (1, HALF - 1)))
    (bands,) = call(toeplitz_kernel, [shape((groups, HALF, 2 * HALF))], [vmem()], (line,), 10**8)

    z, send, head = call(
        gated_kernel,
        [shape((rows, width)), shape((HALF + 3 * TAIL, width)), shape((3 * TAIL, width))],
        [smem(), smem(), vmem(), vmem()],
        (bpd, doc_lengths, blocks, short_filters),
        10**7,
        scratch=[pltpu.VMEM((2, rows + TAIL, width), F32)],
    )
    recv = passed_along(send)
    (query,) = call(
        query_kernel,
        [shape((rows, width), F32)],
        [smem(), smem(), vmem(), vmem()],
        (bpd, doc_lengths, blocks, short_filters),
        10**7,
        scratch=[pltpu.VMEM((rows + TAIL, width), F32)],
    )
    gain = skip_gain.reshape(1, width)
    (copies,) = call(
        hidden_kernel,
        [shape((nx, rows, width))],
        [smem()] + [vmem()] * 7,
        (doc_lengths, z, query, recv, head, short_filters, bands, gain),
        10**9,
        scratch=[pltpu.VMEM((rows + HALF, width), BF16), pltpu.VMEM((HALF, width), F32)],
    )
    own = lax.all_to_all(copies, "x", split_axis=0, concat_axis=0, tiled=True)
    own = own.reshape(nx * rows, width)
    other = lax.ppermute(own, "core", [(0, 1), (1, 0)])
    got = []
    for part, distance in ((0, 1), (1, -1)):
        (cross,) = project((part,), 1, own, other, weights, nx)
        got.append(along_z(cross, distance))
    mine = project((0, 1), 0, own, other, weights, nx)
    nzh, half, _, lane = mine[0].shape
    (pairs,) = call(pair_kernel, [shape((nzh, nx, rows, lane))], [vmem()] * 4, (*mine, *got), 10**6)
    flat = pairs.reshape(nzh * nx, rows, lane)
    parts = lax.all_to_all(flat, ("zh", "x"), split_axis=0, concat_axis=0, tiled=True)
    return summed(parts.reshape(pairs.shape))


def solution(mesh):
    ctx, mp = CTX, ("zh", "zl", "core")
    mesh5 = Mesh(mesh.devices.reshape(SHAPE5), ctx + mp)
    return jax.shard_map(
        operator,
        mesh=mesh5,
        in_specs=(
            P(ctx, None, mp),
            P(None, None, mp),
            P(None, mp),
            P(mp),
            P(mp, ctx),
            P(),
            P(),
        ),
        out_specs=P(ctx, mp),
        check_vma=False,
    )
```

```python
import functools

import jax
import jax.numpy as jnp
from jax import lax
from jax.experimental import pallas as pl
from jax.experimental.pallas import tpu as pltpu
from jax.sharding import Mesh, PartitionSpec as P


CTX = ("y", "x")
SHAPE5 = (8, 4, 4, 2, 2)
BLK = 16
TAIL = 8
GRANT = 24 << 20
HALF = 128
F32, BF16 = jnp.float32, jnp.bfloat16


def smem():
    return pl.BlockSpec(memory_space=pltpu.SMEM)


def vmem():
    return pl.BlockSpec(memory_space=pltpu.VMEM)


def stretch_id():
    return lax.axis_index("y") * lax.axis_size("x") + lax.axis_index("x")


def call(body, outs, ins, args, flops, scratch=()):
    moved = sum(a.size * a.dtype.itemsize for a in args)
    moved += sum(o.size * o.dtype.itemsize for o in outs)
    return pl.pallas_call(
        body,
        out_shape=outs,
        in_specs=ins,
        out_specs=[vmem()] * len(outs),
        scratch_shapes=list(scratch),
        compiler_params=pltpu.CompilerParams(vmem_limit_bytes=GRANT),
        cost_estimate=pl.CostEstimate(flops=flops, bytes_accessed=moved, transcendentals=0),
    )(*args)


def reach_back(lengths, first, shape):
    at = first + lax.broadcasted_iota(jnp.int32, shape, 0)
    begin = jnp.zeros(shape, jnp.int32)
    start = jnp.int32(0)
    for doc in range(lengths.shape[0]):
        begin = jnp.where(at >= start, start, begin)
        start = start + lengths[doc]
    return at - begin


def short_rows(window, taps_ref, which, back):
    count = back.shape[0]
    total = jnp.zeros(back.shape, F32)
    for step in range(taps_ref.shape[1]):
        tap = taps_ref[which, step : step + 1, :].astype(F32)
        piece = window[TAIL - step : TAIL - step + count]
        total = total + jnp.where(back >= step, tap * piece, 0.0)
    return total


def pack_kernel(bpd, src, out, sem):
    me = stretch_id()

    def one(c, slot):
        mine = bpd[0, c] == me
        for k in range(1, bpd.shape[0]):
            mine = mine | (bpd[k, c] == me)
        rows = pl.ds(pl.multiple_of(slot * BLK, BLK), BLK)
        pltpu.make_async_copy(src.at[:, rows, :], out.at[c], sem).start()
        return slot + mine.astype(jnp.int32)

    lax.fori_loop(0, bpd.shape[1], one, jnp.int32(0), unroll=2)
    pltpu.make_async_copy(out, out, sem).wait()


def packed_blocks(bpd, src, stretches):
    return pl.pallas_call(
        pack_kernel,
        in_specs=[smem(), vmem()],
        out_specs=pl.BlockSpec(memory_space=pl.ANY),
        out_shape=shape((stretches, 3, BLK, src.shape[2])),
        scratch_shapes=[pltpu.SemaphoreType.DMA],
        cost_estimate=pl.CostEstimate(
            flops=10**6, bytes_accessed=4 * src.size, transcendentals=0
        ),
        name="pack",
    )(bpd, src)


def toeplitz_kernel(line, out):
    def one(g, carry):
        row = jnp.broadcast_to(line[pl.ds(g, 1), :], out.shape[1:])
        out[g] = pltpu.roll(row, 0, 1, stride=1, stride_axis=0).astype(BF16)
        return carry

    lax.fori_loop(0, out.shape[0], one, 0, unroll=4)


def gather_rows(bpd, blocks, which, buf):
    me = stretch_id()
    buf[0:TAIL, :] = jnp.zeros((TAIL, buf.shape[1]), F32)
    for k in range((buf.shape[0] - TAIL) // BLK):
        buf[TAIL + k * BLK : TAIL + (k + 1) * BLK, :] = blocks[bpd[k, me], which].astype(F32)


STEP = 32


def gated_kernel(bpd, lengths, blocks, taps, z, send, head, buf):
    me = stretch_id()
    rows, width = z.shape
    for i in range(2):
        gather_rows(bpd, blocks, 1 + i, buf.at[i])

    def chunk(r, carry):
        at = pl.multiple_of(r * STEP, STEP)
        back = reach_back(lengths, me * rows + at, (STEP, width))
        wide = pl.ds(at, STEP + TAIL)
        keyed = short_rows(buf[0, wide, :], taps, 1, back)
        valued = short_rows(buf[1, wide, :], taps, 2, back)
        z[pl.ds(at, STEP), :] = (keyed * valued).astype(BF16)
        return carry

    lax.fori_loop(0, rows // STEP, chunk, 0)
    send[0:HALF, :] = z[rows - HALF :, :]
    q_last = blocks[bpd[rows // BLK - 1, me], 0].astype(F32)[BLK - TAIL :]
    q_first = blocks[bpd[0, me], 0].astype(F32)[:TAIL]
    tails = [q_last] + [buf[i, rows : rows + TAIL, :] for i in range(2)]
    heads = [q_first] + [buf[i, TAIL : 2 * TAIL, :] for i in range(2)]
    for i in range(3):
        send[HALF + i * TAIL : HALF + (i + 1) * TAIL, :] = tails[i].astype(BF16)
        head[i * TAIL : (i + 1) * TAIL, :] = heads[i].astype(BF16)


def query_kernel(bpd, lengths, blocks, taps, out, buf):
    me = stretch_id()
    rows, width = out.shape
    gather_rows(bpd, blocks, 0, buf)

    def chunk(r, carry):
        at = pl.multiple_of(r * STEP, STEP)
        back = reach_back(lengths, me * rows + at, (STEP, width))
        out[pl.ds(at, STEP), :] = short_rows(buf[pl.ds(at, STEP + TAIL), :], taps, 0, back)
        return carry

    lax.fori_loop(0, rows // STEP, chunk, 0)


def hidden_kernel(lengths, z, query, recv, head, taps, bands, gain, out, ext, first_q):
    me = stretch_id()
    rows, width = z.shape
    back = reach_back(lengths, me * rows, (TAIL, width))
    fixed = []
    for i in range(3):
        tail = recv[HALF + i * TAIL : HALF + (i + 1) * TAIL, :].astype(F32)
        mine = head[i * TAIL : (i + 1) * TAIL, :].astype(F32)
        fixed.append(short_rows(jnp.concatenate([tail, mine], axis=0), taps, i, back))
    first = (fixed[1] * fixed[2]).astype(BF16).astype(F32)
    ext[0:HALF, :] = recv[0:HALF, :]
    ext[HALF:, :] = z[...]
    later = z[TAIL : 2 * TAIL, :].astype(F32)
    ext[HALF : HALF + 2 * TAIL, :] = jnp.concatenate([first, later], axis=0).astype(BF16)
    first_q[0:TAIL, :] = fixed[0]
    first_q[TAIL:, :] = query[TAIL:HALF, :]
    lane = 128
    per = lane // (width // bands.shape[0])
    group = lax.broadcasted_iota(jnp.int32, (HALF, lane), 1) // (lane // per)
    for b in range(rows // HALF):
        back = reach_back(lengths, me * rows + b * HALF, (HALF, 2 * HALF))
        i = lax.broadcasted_iota(jnp.int32, (HALF, 2 * HALF), 0)
        p = lax.broadcasted_iota(jnp.int32, (HALF, 2 * HALF), 1)
        keep = jnp.where(i + HALF - p <= back, 1.0, 0.0).astype(BF16)
        for t in range(width // lane):
            cols = slice(t * lane, (t + 1) * lane)
            right = ext[b * HALF : (b + 2) * HALF, cols]
            total = jnp.zeros((HALF, lane), F32)
            for g in range(per):
                got = jnp.dot(bands[t * per + g] * keep, right, preferred_element_type=F32)
                total = jnp.where(group == g, got, total)
            zs = ext[(b + 1) * HALF : (b + 2) * HALF, cols].astype(F32)
            q = first_q[:, cols] if b == 0 else query[b * HALF : (b + 1) * HALF, cols]
            value = (q * (total + gain[:, cols] * zs)).astype(BF16)
            for copy in range(out.shape[0]):
                out[copy, b * HALF : (b + 1) * HALF, cols] = value


def relay_kernel(up, down, up_out, down_out):
    up_out[...] = up[...]
    down_out[...] = down[...]


DISTANCES = ((0, 2, -2, 4), (1, -1, 3, -3))


def project_kernel(parts, cross, own, other, *refs):
    block, up, down, up2, down2, up3, down3, up4 = refs[:8]
    outs = refs[8:]
    count, rows, lane = outs[0].shape[1:]
    n = 2 * outs[0].shape[0]
    load = {
        0: lambda: block[...],
        1: lambda: up[...],
        -1: lambda: down[...],
        2: lambda: up2[...],
        -2: lambda: down2[...],
        3: lambda: up3[...],
        -3: lambda: down3[...],
        4: lambda: up4[...],
    }
    y = lax.axis_index("y")
    parity = lax.rem(y + lax.axis_index("zl"), 2)

    def fill(distances):
        for part, out in zip(parts, outs):
            at = slice(part * count * rows, (part + 1) * count * rows)
            left = jnp.concatenate([own[at, :], other[at, :]], axis=1)
            for pair in (distances[:2], distances[2:]):
                wide = jnp.concatenate([load[d]() for d in pair], axis=1)
                got = jnp.dot(left, wide, preferred_element_type=F32).astype(BF16)
                for i, d in enumerate(pair):
                    high = lax.div(lax.rem(y - d + n, n), 2)
                    piece = got[:, i * lane : (i + 1) * lane]
                    out[high] = piece.reshape(count, rows, lane)

    for odd in range(2):

        @pl.when(lax.rem(parity + odd, 2) == cross)
        def _():
            fill(DISTANCES[odd])


def project(parts, cross, own, other, weights, nx):
    rows = own.shape[0] // nx
    lane = weights[0].shape[1]
    return call(
        functools.partial(project_kernel, parts, cross),
        [shape((len(DISTANCES[0]), nx // 2, rows, lane))] * len(parts),
        [vmem()] * (2 + len(weights)),
        (own, other, *weights),
        4 * own.size * 2 * len(parts) * lane,
    )


def pair_kernel(own0, own1, got0, got1, out):
    count = own0.shape[1]

    def one(z, carry):
        for i, (own, got) in enumerate(((own0, got0), (own1, got1))):
            for s in range(count):
                total = own[z, s].astype(F32) + got[z, s].astype(F32)
                out[z, i * count + s] = total.astype(BF16)
        return carry

    lax.fori_loop(0, own0.shape[0], one, 0)


def along_z(block, distance):
    n = lax.axis_size(("zh", "zl"))
    return lax.ppermute(block, ("zh", "zl"), [(i, (i + distance) % n) for i in range(n)])


def summed(parts):
    columns = [jnp.sum(parts[:, x].astype(F32), axis=0) for x in range(parts.shape[1])]
    return jnp.concatenate(columns, axis=1).astype(BF16)


def shape(dims, dtype=BF16):
    return jax.ShapeDtypeStruct(dims, dtype)


def passed_along(block):
    n = lax.axis_size(CTX)
    return lax.ppermute(block, CTX, [(i, i + 1) for i in range(n - 1)])


def weight_columns(out_weight):
    nx = lax.axis_size("x")
    core = lax.axis_index("core")
    width = out_weight.shape[1] // 2
    halves = (out_weight[:, :width], out_weight[:, width:])
    same = jnp.where(core == 0, halves[0], halves[1])
    flip = jnp.where(core == 0, halves[1], halves[0])
    route = lambda f: [
        (x * 2 + i, (2 * (x % 2) + f(i)) * 2 + x // 2) for x in range(nx) for i in range(2)
    ]
    a = lax.ppermute(same, ("x", "core"), route(lambda i: i))
    b = lax.ppermute(flip, ("x", "core"), route(lambda i: 1 - i))
    straight = lax.axis_index("x") % 2 == core
    own = jnp.where(straight, a, b)
    other = jnp.where(straight, b, a)
    return jnp.concatenate([own, other], axis=0)


def around(block, distance):
    n = lax.axis_size("y")
    return lax.ppermute(block, "y", [(i, (i + distance) % n) for i in range(n)])


def operator(
    source_rows,
    short_filters,
    medium_filters,
    skip_gain,
    out_weight,
    doc_lengths,
    block_packing_device,
):
    ny, nx = lax.axis_size("y"), lax.axis_size("x")
    stretches = ny * nx
    width = source_rows.shape[2]
    rows = block_packing_device.shape[1] * BLK
    bpd = block_packing_device.T

    packed = packed_blocks(bpd, source_rows.transpose(1, 0, 2), stretches)
    blocks = lax.all_to_all(packed, CTX, split_axis=0, concat_axis=0, tiled=True)

    block = weight_columns(out_weight)
    up, down = around(block, 1), around(block, -1)
    up2, down2 = around(up, 1), around(down, -1)
    both = [shape(block.shape)] * 2
    far_up, far_down = call(relay_kernel, both, [vmem()] * 2, (up2, down2), 0)
    up4 = around(far_up, 2)
    up3, down3 = around(far_up, 1), around(far_down, -1)
    weights = (block, up, down, up2, down2, up3, down3, up4)

    groups = medium_filters.shape[1]
    line = jnp.pad(medium_filters[::-1].T.astype(F32), ((0, 0), (1, HALF - 1)))
    (bands,) = call(toeplitz_kernel, [shape((groups, HALF, 2 * HALF))], [vmem()], (line,), 10**8)

    z, send, head = call(
        gated_kernel,
        [shape((rows, width)), shape((HALF + 3 * TAIL, width)), shape((3 * TAIL, width))],
        [smem(), smem(), vmem(), vmem()],
        (bpd, doc_lengths, blocks, short_filters),
        10**7,
        scratch=[pltpu.VMEM((2, rows + TAIL, width), F32)],
    )
    recv = passed_along(send)
    (query,) = call(
        query_kernel,
        [shape((rows, width), F32)],
        [smem(), smem(), vmem(), vmem()],
        (bpd, doc_lengths, blocks, short_filters),
        10**7,
        scratch=[pltpu.VMEM((rows + TAIL, width), F32)],
    )
    gain = skip_gain.reshape(1, width)
    (copies,) = call(
        hidden_kernel,
        [shape((nx, rows, width))],
        [smem()] + [vmem()] * 7,
        (doc_lengths, z, query, recv, head, short_filters, bands, gain),
        10**9,
        scratch=[pltpu.VMEM((rows + HALF, width), BF16), pltpu.VMEM((HALF, width), F32)],
    )
    own = lax.all_to_all(copies, "x", split_axis=0, concat_axis=0, tiled=True)
    own = own.reshape(nx * rows, width)
    other = lax.ppermute(own, "core", [(0, 1), (1, 0)])
    got = []
    for part, distance in ((0, 1), (1, -1)):
        (cross,) = project((part,), 1, own, other, weights, nx)
        got.append(along_z(cross, distance))
    mine = project((0, 1), 0, own, other, weights, nx)
    nzh, _, _, lane = mine[0].shape
    (pairs,) = call(pair_kernel, [shape((nzh, nx, rows, lane))], [vmem()] * 4, (*mine, *got), 10**6)
    flat = pairs.reshape(nzh * nx, rows, lane)
    parts = lax.all_to_all(flat, ("zh", "x"), split_axis=0, concat_axis=0, tiled=True)
    return summed(parts.reshape(pairs.shape))


def solution(mesh):
    ctx, mp = CTX, ("zh", "zl", "core")
    mesh5 = Mesh(mesh.devices.reshape(SHAPE5), ctx + mp)
    return jax.shard_map(
        operator,
        mesh=mesh5,
        in_specs=(
            P(ctx, None, mp),
            P(None, None, mp),
            P(None, mp),
            P(mp),
            P(mp, ctx),
            P(),
            P(),
        ),
        out_specs=P(ctx, mp),
        check_vma=False,
    )
```

```python
import functools

import jax
import jax.numpy as jnp
from jax import lax
from jax.experimental import pallas as pl
from jax.experimental.pallas import tpu as pltpu
from jax.sharding import Mesh, PartitionSpec as P


CTX = ("y", "x")
SHAPE5 = (8, 4, 4, 2, 2)
BLK = 16
TAIL = 8
GRANT = 24 << 20
HALF = 128
F32, BF16 = jnp.float32, jnp.bfloat16


def smem():
    return pl.BlockSpec(memory_space=pltpu.SMEM)


def vmem():
    return pl.BlockSpec(memory_space=pltpu.VMEM)


def stretch_id():
    return lax.axis_index("y") * lax.axis_size("x") + lax.axis_index("x")


def call(body, outs, ins, args, flops, scratch=()):
    moved = sum(a.size * a.dtype.itemsize for a in args)
    moved += sum(o.size * o.dtype.itemsize for o in outs)
    return pl.pallas_call(
        body,
        out_shape=outs,
        in_specs=ins,
        out_specs=[vmem()] * len(outs),
        scratch_shapes=list(scratch),
        compiler_params=pltpu.CompilerParams(vmem_limit_bytes=GRANT),
        cost_estimate=pl.CostEstimate(flops=flops, bytes_accessed=moved, transcendentals=0),
    )(*args)


def reach_back(lengths, first, shape):
    at = first + lax.broadcasted_iota(jnp.int32, shape, 0)
    begin = jnp.zeros(shape, jnp.int32)
    start = jnp.int32(0)
    for doc in range(lengths.shape[0]):
        begin = jnp.where(at >= start, start, begin)
        start = start + lengths[doc]
    return at - begin


def short_rows(window, taps_ref, which, back):
    count = back.shape[0]
    total = jnp.zeros(back.shape, F32)
    for step in range(taps_ref.shape[1]):
        tap = taps_ref[which, step : step + 1, :].astype(F32)
        piece = window[TAIL - step : TAIL - step + count]
        total = total + jnp.where(back >= step, tap * piece, 0.0)
    return total


def pack_kernel(bpd, src, out, sem):
    me = stretch_id()

    def one(c, slot):
        mine = bpd[0, c] == me
        for k in range(1, bpd.shape[0]):
            mine = mine | (bpd[k, c] == me)
        rows = pl.ds(pl.multiple_of(slot * BLK, BLK), BLK)
        pltpu.make_async_copy(src.at[:, rows, :], out.at[c], sem).start()
        return slot + mine.astype(jnp.int32)

    lax.fori_loop(0, bpd.shape[1], one, jnp.int32(0), unroll=2)
    pltpu.make_async_copy(out, out, sem).wait()


def packed_blocks(bpd, src, stretches):
    return pl.pallas_call(
        pack_kernel,
        in_specs=[smem(), vmem()],
        out_specs=pl.BlockSpec(memory_space=pl.ANY),
        out_shape=shape((stretches, 3, BLK, src.shape[2])),
        scratch_shapes=[pltpu.SemaphoreType.DMA],
        cost_estimate=pl.CostEstimate(
            flops=10**6, bytes_accessed=4 * src.size, transcendentals=0
        ),
        name="pack",
    )(bpd, src)


def toeplitz_kernel(line, out):
    def one(g, carry):
        row = jnp.broadcast_to(line[pl.ds(g, 1), :], out.shape[1:])
        out[g] = pltpu.roll(row, 0, 1, stride=1, stride_axis=0).astype(BF16)
        return carry

    lax.fori_loop(0, out.shape[0], one, 0, unroll=4)


def gather_rows(bpd, blocks, which, buf):
    me = stretch_id()
    buf[0:TAIL, :] = jnp.zeros((TAIL, buf.shape[1]), F32)
    for k in range((buf.shape[0] - TAIL) // BLK):
        buf[TAIL + k * BLK : TAIL + (k + 1) * BLK, :] = blocks[bpd[k, me], which].astype(F32)


STEP = 32


def gated_kernel(bpd, lengths, blocks, taps, z, send, head, buf):
    me = stretch_id()
    rows, width = z.shape
    for i in range(2):
        gather_rows(bpd, blocks, 1 + i, buf.at[i])

    def chunk(r, carry):
        at = pl.multiple_of(r * STEP, STEP)
        back = reach_back(lengths, me * rows + at, (STEP, width))
        wide = pl.ds(at, STEP + TAIL)
        keyed = short_rows(buf[0, wide, :], taps, 1, back)
        valued = short_rows(buf[1, wide, :], taps, 2, back)
        z[pl.ds(at, STEP), :] = (keyed * valued).astype(BF16)
        return carry

    lax.fori_loop(0, rows // STEP, chunk, 0)
    send[0:HALF, :] = z[rows - HALF :, :]
    q_last = blocks[bpd[rows // BLK - 1, me], 0].astype(F32)[BLK - TAIL :]
    q_first = blocks[bpd[0, me], 0].astype(F32)[:TAIL]
    tails = [q_last] + [buf[i, rows : rows + TAIL, :] for i in range(2)]
    heads = [q_first] + [buf[i, TAIL : 2 * TAIL, :] for i in range(2)]
    for i in range(3):
        send[HALF + i * TAIL : HALF + (i + 1) * TAIL, :] = tails[i].astype(BF16)
        head[i * TAIL : (i + 1) * TAIL, :] = heads[i].astype(BF16)


def query_kernel(bpd, lengths, blocks, taps, out, buf):
    me = stretch_id()
    rows, width = out.shape
    gather_rows(bpd, blocks, 0, buf)

    def chunk(r, carry):
        at = pl.multiple_of(r * STEP, STEP)
        back = reach_back(lengths, me * rows + at, (STEP, width))
        out[pl.ds(at, STEP), :] = short_rows(buf[pl.ds(at, STEP + TAIL), :], taps, 0, back)
        return carry

    lax.fori_loop(0, rows // STEP, chunk, 0)


def hidden_kernel(lengths, z, query, recv, head, taps, bands, gain, out, ext, first_q):
    me = stretch_id()
    rows, width = z.shape
    back = reach_back(lengths, me * rows, (TAIL, width))
    fixed = []
    for i in range(3):
        tail = recv[HALF + i * TAIL : HALF + (i + 1) * TAIL, :].astype(F32)
        mine = head[i * TAIL : (i + 1) * TAIL, :].astype(F32)
        fixed.append(short_rows(jnp.concatenate([tail, mine], axis=0), taps, i, back))
    first = (fixed[1] * fixed[2]).astype(BF16).astype(F32)
    ext[0:HALF, :] = recv[0:HALF, :]
    ext[HALF:, :] = z[...]
    later = z[TAIL : 2 * TAIL, :].astype(F32)
    ext[HALF : HALF + 2 * TAIL, :] = jnp.concatenate([first, later], axis=0).astype(BF16)
    first_q[0:TAIL, :] = fixed[0]
    first_q[TAIL:, :] = query[TAIL:HALF, :]
    lane = 128
    per = lane // (width // bands.shape[0])
    group = lax.broadcasted_iota(jnp.int32, (HALF, lane), 1) // (lane // per)
    for b in range(rows // HALF):
        back = reach_back(lengths, me * rows + b * HALF, (HALF, 2 * HALF))
        i = lax.broadcasted_iota(jnp.int32, (HALF, 2 * HALF), 0)
        p = lax.broadcasted_iota(jnp.int32, (HALF, 2 * HALF), 1)
        keep = jnp.where(i + HALF - p <= back, 1.0, 0.0).astype(BF16)
        for t in range(width // lane):
            cols = slice(t * lane, (t + 1) * lane)
            right = ext[b * HALF : (b + 2) * HALF, cols]
            total = jnp.zeros((HALF, lane), F32)
            for g in range(per):
                got = jnp.dot(bands[t * per + g] * keep, right, preferred_element_type=F32)
                total = jnp.where(group == g, got, total)
            zs = ext[(b + 1) * HALF : (b + 2) * HALF, cols].astype(F32)
            q = first_q[:, cols] if b == 0 else query[b * HALF : (b + 1) * HALF, cols]
            value = (q * (total + gain[:, cols] * zs)).astype(BF16)
            for copy in range(out.shape[0]):
                out[copy, b * HALF : (b + 1) * HALF, cols] = value


def relay_kernel(up, down, up_out, down_out, up_half, down_half):
    rows = up_half.shape[0]
    up_out[...] = up[...]
    down_out[...] = down[...]
    up_half[...] = up[:rows]
    down_half[...] = down[rows:]


DISTANCES = ((0, 2, -2, 4), (1, -1, 3, -3))


def project_kernel(parts, cross, own, other, *refs):
    block, up, down, up2, down2, up3, down3, up4, down4 = refs[:9]
    outs = refs[9:]
    count, rows, lane = outs[0].shape[1:]
    n = 2 * outs[0].shape[0]
    load = {
        0: lambda: block[...],
        1: lambda: up[...],
        -1: lambda: down[...],
        2: lambda: up2[...],
        -2: lambda: down2[...],
        3: lambda: up3[...],
        -3: lambda: down3[...],
        4: lambda: jnp.concatenate([up4[...], down4[...]], axis=0),
    }
    y = lax.axis_index("y")
    parity = lax.rem(y + lax.axis_index("zl"), 2)

    def fill(distances):
        for part, out in zip(parts, outs):
            at = slice(part * count * rows, (part + 1) * count * rows)
            left = jnp.concatenate([own[at, :], other[at, :]], axis=1)
            for pair in (distances[:2], distances[2:]):
                wide = jnp.concatenate([load[d]() for d in pair], axis=1)
                got = jnp.dot(left, wide, preferred_element_type=F32).astype(BF16)
                for i, d in enumerate(pair):
                    high = lax.div(lax.rem(y - d + n, n), 2)
                    piece = got[:, i * lane : (i + 1) * lane]
                    out[high] = piece.reshape(count, rows, lane)

    for odd in range(2):

        @pl.when(lax.rem(parity + odd, 2) == cross)
        def _():
            fill(DISTANCES[odd])


def project(parts, cross, own, other, weights, nx):
    rows = own.shape[0] // nx
    lane = weights[0].shape[1]
    return call(
        functools.partial(project_kernel, parts, cross),
        [shape((len(DISTANCES[0]), nx // 2, rows, lane))] * len(parts),
        [vmem()] * (2 + len(weights)),
        (own, other, *weights),
        4 * own.size * 2 * len(parts) * lane,
    )


def pair_kernel(own0, own1, got0, got1, out):
    count = own0.shape[1]

    def one(z, carry):
        for i, (own, got) in enumerate(((own0, got0), (own1, got1))):
            for s in range(count):
                total = own[z, s].astype(F32) + got[z, s].astype(F32)
                out[z, i * count + s] = total.astype(BF16)
        return carry

    lax.fori_loop(0, own0.shape[0], one, 0)


def along_z(block, distance):
    n = lax.axis_size(("zh", "zl"))
    return lax.ppermute(block, ("zh", "zl"), [(i, (i + distance) % n) for i in range(n)])


def summed(parts):
    columns = [jnp.sum(parts[:, x].astype(F32), axis=0) for x in range(parts.shape[1])]
    return jnp.concatenate(columns, axis=1).astype(BF16)


def shape(dims, dtype=BF16):
    return jax.ShapeDtypeStruct(dims, dtype)


def passed_along(block):
    n = lax.axis_size(CTX)
    return lax.ppermute(block, CTX, [(i, i + 1) for i in range(n - 1)])


def weight_columns(out_weight):
    nx = lax.axis_size("x")
    core = lax.axis_index("core")
    width = out_weight.shape[1] // 2
    halves = (out_weight[:, :width], out_weight[:, width:])
    same = jnp.where(core == 0, halves[0], halves[1])
    flip = jnp.where(core == 0, halves[1], halves[0])
    route = lambda f: [
        (x * 2 + i, (2 * (x % 2) + f(i)) * 2 + x // 2) for x in range(nx) for i in range(2)
    ]
    a = lax.ppermute(same, ("x", "core"), route(lambda i: i))
    b = lax.ppermute(flip, ("x", "core"), route(lambda i: 1 - i))
    straight = lax.axis_index("x") % 2 == core
    own = jnp.where(straight, a, b)
    other = jnp.where(straight, b, a)
    return jnp.concatenate([own, other], axis=0)


def around(block, distance):
    n = lax.axis_size("y")
    return lax.ppermute(block, "y", [(i, (i + distance) % n) for i in range(n)])


def operator(
    source_rows,
    short_filters,
    medium_filters,
    skip_gain,
    out_weight,
    doc_lengths,
    block_packing_device,
):
    ny, nx = lax.axis_size("y"), lax.axis_size("x")
    stretches = ny * nx
    width = source_rows.shape[2]
    rows = block_packing_device.shape[1] * BLK
    bpd = block_packing_device.T

    packed = packed_blocks(bpd, source_rows.transpose(1, 0, 2), stretches)
    blocks = lax.all_to_all(packed, CTX, split_axis=0, concat_axis=0, tiled=True)

    block = weight_columns(out_weight)
    up, down = around(block, 1), around(block, -1)
    up2, down2 = around(up, 1), around(down, -1)
    whole = shape(block.shape)
    half = shape((block.shape[0] // 2, block.shape[1]))
    far_up, far_down, up_half, down_half = call(
        relay_kernel, [whole, whole, half, half], [vmem()] * 2, (up2, down2), 0
    )
    up4, down4 = around(up_half, 2), around(down_half, -2)
    up3, down3 = around(far_up, 1), around(far_down, -1)
    weights = (block, up, down, up2, down2, up3, down3, up4, down4)

    groups = medium_filters.shape[1]
    line = jnp.pad(medium_filters[::-1].T.astype(F32), ((0, 0), (1, HALF - 1)))
    (bands,) = call(toeplitz_kernel, [shape((groups, HALF, 2 * HALF))], [vmem()], (line,), 10**8)

    z, send, head = call(
        gated_kernel,
        [shape((rows, width)), shape((HALF + 3 * TAIL, width)), shape((3 * TAIL, width))],
        [smem(), smem(), vmem(), vmem()],
        (bpd, doc_lengths, blocks, short_filters),
        10**7,
        scratch=[pltpu.VMEM((2, rows + TAIL, width), F32)],
    )
    recv = passed_along(send)
    (query,) = call(
        query_kernel,
        [shape((rows, width), F32)],
        [smem(), smem(), vmem(), vmem()],
        (bpd, doc_lengths, blocks, short_filters),
        10**7,
        scratch=[pltpu.VMEM((rows + TAIL, width), F32)],
    )
    gain = skip_gain.reshape(1, width)
    (copies,) = call(
        hidden_kernel,
        [shape((nx, rows, width))],
        [smem()] + [vmem()] * 7,
        (doc_lengths, z, query, recv, head, short_filters, bands, gain),
        10**9,
        scratch=[pltpu.VMEM((rows + HALF, width), BF16), pltpu.VMEM((HALF, width), F32)],
    )
    own = lax.all_to_all(copies, "x", split_axis=0, concat_axis=0, tiled=True)
    own = own.reshape(nx * rows, width)
    other = lax.ppermute(own, "core", [(0, 1), (1, 0)])
    got = []
    for part, distance in ((0, 1), (1, -1)):
        (cross,) = project((part,), 1, own, other, weights, nx)
        got.append(along_z(cross, distance))
    mine = project((0, 1), 0, own, other, weights, nx)
    nzh, half, _, lane = mine[0].shape
    (pairs,) = call(pair_kernel, [shape((nzh, nx, rows, lane))], [vmem()] * 4, (*mine, *got), 10**6)
    flat = pairs.reshape(nzh * nx, rows, lane)
    parts = lax.all_to_all(flat, ("zh", "x"), split_axis=0, concat_axis=0, tiled=True)
    return summed(parts.reshape(pairs.shape))


def solution(mesh):
    ctx, mp = CTX, ("zh", "zl", "core")
    mesh5 = Mesh(mesh.devices.reshape(SHAPE5), ctx + mp)
    return jax.shard_map(
        operator,
        mesh=mesh5,
        in_specs=(
            P(ctx, None, mp),
            P(None, None, mp),
            P(None, mp),
            P(mp),
            P(mp, ctx),
            P(),
            P(),
        ),
        out_specs=P(ctx, mp),
        check_vma=False,
    )
```
